32 devices in a mesh: expert: 8 (over y, x, core), dp: 4 (over z).
Axes of the slice: x: 2, y: 2, z: 4, core: 2. Of those that a mesh axis runs over, the one named last changes fastest.
Arguments:
- tokens: bfloat16 [4096, 2048], P(('expert', 'dp')), may hold values from -6 to 6
- cotangent: bfloat16 [4096, 2048], P(('expert', 'dp')), may hold values from -6 to 6
- expert_ids: int32 [4096, 8], P(('expert', 'dp')), may hold values from 0 to 31, all different within a row; in each aligned block of 128 rows (0 to 127, 128 to 255, ...) at most 40 rows name the same one
- combine_weights: float32 [4096, 8], P(('expert', 'dp')), may hold values from 0.1 to 1
- w_gate: bfloat16 [32, 2048, 384], P('expert'), may hold values from -0.125 to 0.125
- w_up: bfloat16 [32, 2048, 384], P('expert'), may hold values from -0.125 to 0.125
- w_down: bfloat16 [32, 2048, 384], P('expert'), may hold values from -0.3125 to 0.3125
- swap_flags: int32 [4], replicated, may hold values 0 or 1
Outputs:
- mixed: bfloat16 [4096, 2048], P(('expert', 'dp'))
- input_grad: bfloat16 [4096, 2048], P(('expert', 'dp'))
- grad_gate: bfloat16 [32, 2048, 384], P('expert', 'dp')
- grad_up: bfloat16 [32, 2048, 384], P('expert', 'dp')
- grad_down: bfloat16 [32, 2048, 384], P('expert', 'dp')
The draws below stay inside these ranges and needn't reach their ends.
Inputs may be any that keep to these rules, and one draw needn't show every extreme that they name: `expert_ids`: in each aligned block of 128 token rows (the rows of one device) no expert is named by more than 40 rows, a bound that some block reaches. `swap_flags`: entry j concerns the pair of expert-axis indices j and j + 4.
All inputs are finite; a program needn't handle non-finite values.
Results may differ from the reference program's by a relative error of at most 0.0095.
Values may be sent and summed in bfloat16 or wider, within the bound.
A program may use at most 192 MiB of HBM per device.

```python
import math
import jax
import jax.numpy as jnp
import numpy as np
from jax import lax

D = 2048
FW = 384
TOPK = 8
EXP_DEV = 4
TOK_DEV = 128
EXPERTS = 32
TOKENS = 4096
CAP = 40
HALF = 4
N_EXPERT = 8
N_DP = 4


def touch_ends(values, key, low, top_value):
    extent = values.shape
    index_at = [jax.random.randint(jax.random.fold_in(key, axis), (), 0, extent[axis]) for axis in range(len(extent))]
    values = values.at[tuple(index_at)].set(low)
    longest = extent.index(max(extent))
    index_at[longest] = (index_at[longest] + 1) % extent[longest]
    return values.at[tuple(index_at)].set(top_value)


def steps_of(rng, shape, shards, smallest, largest):
    def one(axis_at, blocks):
        heights = jax.random.uniform(jax.random.fold_in(jax.random.fold_in(rng, 6), axis_at), (blocks,), jnp.float32, smallest / len(shards), largest / len(shards))
        return jnp.repeat(jnp.exp(heights), shape[axis_at] // blocks).reshape((-1,) + (1,) * (len(shape) - axis_at - 1))

    factor_of = one(*shards[0])
    for cut in shards[1:]:
        factor_of = factor_of * one(*cut)
    return factor_of


def assign_block(stream_key, own, number, rows, amount, top, reach, slope):
    sequence = jax.random.permutation(stream_key, amount)
    packed, common = shares(amount, rows * top, reach, slope, True), shares(amount, rows * top, reach, slope, False)
    places = jnp.arange(amount)

    def named(sizes, rotation):
        used = int((sizes > 0).sum())
        fixed = max(1, used // 4)
        moved = fixed + (places - fixed + rotation * (used - fixed)) % max(1, amount - fixed)
        return jnp.zeros((amount,), jnp.int32).at[sequence[jnp.where(places < fixed, places, moved)]].set(jnp.asarray(sizes, jnp.int32))

    sizes = jnp.where(number % 4 == 0, named(packed, number // 4), named(common, number - number // 4 - 1))
    mixed = jax.random.permutation(jax.random.fold_in(own, 3), amount)
    source_of, taker = mixed[0:amount // 2 * 2:2], mixed[1:amount // 2 * 2:2]
    slack = jnp.minimum(sizes[source_of] - 1, reach - sizes[taker]) // 2
    slack = jnp.where((source_of == sequence[0]) | (taker == sequence[0]) | (sizes[taker] == 0), 0, jnp.maximum(slack, 0))
    moved = jax.random.randint(jax.random.fold_in(own, 4), (amount // 2,), 0, 1 << 20) % (slack + 1)
    sizes = sizes.at[source_of].add(-moved).at[taker].add(moved)
    members = jnp.searchsorted(jnp.cumsum(sizes), jnp.arange(rows * top), side="right").astype(jnp.int32)
    listing = members.reshape(top, rows).T
    listing = listing[jax.random.permutation(jax.random.fold_in(own, 1), rows)]
    rotation = jax.random.randint(jax.random.fold_in(own, 2), (rows, 1), 0, top)
    return jnp.take_along_axis(listing, (jnp.arange(top)[None, :] + rotation) % top, axis=1)


def shares(count, total, limit, slope, full):
    weights = [(1 << 20) // math.isqrt(rank ** slope) + 1 for rank in range(1, count + 1)]
    largest = limit if full else min(limit, max(-(-total // count), total * weights[0] // sum(weights)))
    least = 1 if total - largest >= count - 1 else 0
    holding, surplus = [largest] + [least] * (count - 1), total - largest - least * (count - 1)
    while surplus > 0:
        candidates = [i for i in range(1, count) if holding[i] < largest] or [i for i in range(1, count) if holding[i] < limit]
        mass, left = sum([weights[i] for i in candidates]), surplus
        for i in candidates:
            more = min(limit - holding[i], max(1, left * weights[i] // mass), surplus)
            holding[i] = holding[i] + more
            surplus = surplus - more
    return np.array(holding)


def centred(stream_key, shape, width, reach, split=(), kind=jnp.bfloat16):
    result = width * jax.random.normal(stream_key, shape, jnp.float32)
    if split:
        result = result * steps_of(stream_key, shape, split, -0.22, 0.18)
    return jnp.clip(result, -reach, reach).astype(kind)


def setup_inputs(seed: int = 0) -> dict:
    key_of = jax.random.split(jax.random.key(seed), 9)
    tokens = centred(key_of[0], (TOKENS, D), 1.0, 6.0, ((0, 32),))
    cotangent = centred(key_of[1], (TOKENS, D), 1.0, 6.0, ((0, 32),))
    expert_ids_keys = jax.random.split(jax.random.fold_in(key_of[2], 1), TOKENS // TOK_DEV)
    expert_ids_turns = jax.random.permutation(jax.random.fold_in(key_of[2], 3), TOKENS // TOK_DEV)
    expert_ids = jax.vmap(lambda own, number: assign_block(jax.random.fold_in(key_of[2], 2), own, number, TOK_DEV, EXPERTS, TOPK, CAP, 2))(expert_ids_keys, expert_ids_turns).reshape((TOKENS, TOPK))
    combine_weights = jnp.clip(jnp.exp(math.log(1.0) - 2.3025851 * jax.random.uniform(key_of[3], (TOKENS, TOPK), jnp.float32) ** steps_of(key_of[3], (TOKENS, TOPK), ((0, 32),), -0.2, 0.2)), 0.1, 1.0)
    w_gate = centred(key_of[4], (EXPERTS, D, FW), D ** -0.5, 0.125, ((0, 8),))
    w_up = centred(key_of[5], (EXPERTS, D, FW), D ** -0.5, 0.125, ((0, 8),))
    w_down = centred(key_of[6], (EXPERTS, D, FW), FW ** -0.5, 0.3125, ((0, 8),))
    swap_flags = touch_ends((jax.random.randint(key_of[7], (HALF,), 0, 2) < 1).astype(jnp.int32), jax.random.fold_in(key_of[7], 1), 0, 1)
    return dict(tokens=tokens, cotangent=cotangent, expert_ids=expert_ids, combine_weights=combine_weights, w_gate=w_gate, w_up=w_up, w_down=w_down, swap_flags=swap_flags)


def reference(tokens, cotangent, expert_ids, combine_weights, w_gate, w_up, w_down, swap_flags):
    route_count = TOKENS * TOPK
    flat_expert = expert_ids.reshape(route_count).astype(jnp.int32)
    route_token = jnp.arange(route_count, dtype=jnp.int32) // TOPK
    route_group = (route_token // TOK_DEV) % N_DP
    sort_keys = route_group * EXPERTS + flat_expert
    order = jnp.argsort(sort_keys, stable=True).astype(jnp.int32)
    sorted_keys = sort_keys[order]
    key_range = jnp.arange(N_DP * EXPERTS, dtype=jnp.int32)
    starts = jnp.searchsorted(sorted_keys, key_range, side="left").astype(jnp.int32)
    ends = jnp.searchsorted(sorted_keys, key_range, side="right").astype(jnp.int32)
    most_rows = N_EXPERT * CAP
    flat_weight = combine_weights.reshape(route_count)

    def per_expert(carry, expert):
        out_acc, grad_acc = carry
        gate_w = w_gate[expert]
        up_w = w_up[expert]
        down_w = w_down[expert]
        grad_sums = [jnp.zeros((D, FW), jnp.float32) for index in range(3)]
        for group in range(N_DP):
            key_now = group * EXPERTS + expert
            position = starts[key_now] + jnp.arange(most_rows, dtype=jnp.int32)
            valid = position < ends[key_now]
            route = order[jnp.minimum(position, route_count - 1)]
            token = route // TOPK
            rows = jnp.where(valid[:, None], tokens[token], jnp.zeros((), jnp.bfloat16))
            gate_pre = jnp.dot(rows, gate_w, preferred_element_type=jnp.float32)
            up_pre = jnp.dot(rows, up_w, preferred_element_type=jnp.float32)
            sigma = jax.nn.sigmoid(gate_pre)
            hidden = (gate_pre * sigma * up_pre).astype(jnp.bfloat16)
            expert_out = jnp.dot(hidden, down_w.T, preferred_element_type=jnp.float32).astype(jnp.bfloat16)
            weight_now = jnp.where(valid, flat_weight[route], jnp.zeros((), jnp.float32))
            out_acc = out_acc.at[token].add(weight_now[:, None] * expert_out.astype(jnp.float32))
            route_cot = (weight_now[:, None] * cotangent[token].astype(jnp.float32)).astype(jnp.bfloat16)
            hidden_cot = jnp.dot(route_cot, down_w, preferred_element_type=jnp.float32)
            gate_cot = (hidden_cot * up_pre * sigma * (1.0 + gate_pre * (1.0 - sigma))).astype(jnp.bfloat16)
            up_cot = (hidden_cot * gate_pre * sigma).astype(jnp.bfloat16)
            input_term = (jnp.dot(gate_cot, gate_w.T, preferred_element_type=jnp.float32)
                          + jnp.dot(up_cot, up_w.T, preferred_element_type=jnp.float32)).astype(jnp.bfloat16)
            grad_acc = grad_acc.at[token].add(jnp.where(valid[:, None], input_term.astype(jnp.float32), jnp.zeros((), jnp.float32)))
            partials = (jnp.dot(rows.T, gate_cot, preferred_element_type=jnp.float32),
                        jnp.dot(rows.T, up_cot, preferred_element_type=jnp.float32),
                        jnp.dot(route_cot.T, hidden, preferred_element_type=jnp.float32))
            for index in range(3):
                rounded = lax.optimization_barrier(partials[index].astype(jnp.bfloat16))
                grad_sums[index] = grad_sums[index] + rounded.astype(jnp.float32)
        return (out_acc, grad_acc), tuple(total.astype(jnp.bfloat16) for total in grad_sums)

    start_carry = (jnp.zeros((TOKENS, D), jnp.float32), jnp.zeros((TOKENS, D), jnp.float32))
    (out_acc, grad_acc), grads = lax.scan(per_expert, start_carry, jnp.arange(EXPERTS, dtype=jnp.int32))
    places = jnp.arange(EXPERTS, dtype=jnp.int32)
    holder = places // EXP_DEV
    position_in = places % EXP_DEV
    flagged = swap_flags[holder % HALF] == 1
    moved = flagged & (position_in == EXP_DEV - 1)
    source = jnp.where(moved, ((holder + HALF) % N_EXPERT) * EXP_DEV + position_in, places).astype(jnp.int32)
    return (out_acc.astype(jnp.bfloat16), grad_acc.astype(jnp.bfloat16),
            grads[0][source], grads[1][source], grads[2][source])
```

```python
import functools

import jax
import jax.numpy as jnp
from jax import lax
from jax.experimental import pallas as pl
from jax.experimental.pallas import tpu as pltpu
from jax.sharding import PartitionSpec as P

F32 = jnp.float32
BF16 = jnp.bfloat16
VMEM_BYTES = 56 * 1024 * 1024


def dot(a, b, dims):
    return lax.dot_general(a, b, (dims, ((), ())), preferred_element_type=F32)


def forward_kernel(slot_ref, x_ref, wg_ref, wu_ref, wd_ref, out_ref, hid_ref, dgate_ref, dup_ref):
    x = x_ref[...]
    gate = dot(x, wg_ref[...], ((1,), (0,)))
    up = dot(x, wu_ref[...], ((1,), (0,)))
    s = jax.nn.sigmoid(gate)
    silu = gate * s
    hidden = (silu * up).astype(BF16)
    hid_ref[...] = hidden
    dgate_ref[...] = up * s * (1.0 + gate * (1.0 - s))
    dup_ref[...] = silu
    out_ref[...] = dot(hidden, wd_ref[...], ((1,), (1,))).astype(BF16)


def backward_kernel(
    slot_ref, c_ref, dgate_ref, dup_ref, wg_ref, wu_ref, wd_ref, term_ref, gc_ref, uc_ref
):
    hidden_cot = dot(c_ref[...], wd_ref[...], ((1,), (0,)))
    gate_cot = (hidden_cot * dgate_ref[...]).astype(BF16)
    up_cot = (hidden_cot * dup_ref[...]).astype(BF16)
    gc_ref[...] = gate_cot
    uc_ref[...] = up_cot
    term_ref[...] = (
        dot(gate_cot, wg_ref[...], ((1,), (1,))) + dot(up_cot, wu_ref[...], ((1,), (1,)))
    ).astype(BF16)


def grads_kernel(lhs_ref, *refs):
    lhs = lhs_ref[...]
    out_ref = refs[-1]
    for k, right_ref in enumerate(refs[:-1]):
        out_ref[0, k] = dot(lhs, right_ref[...], ((0,), (0,))).astype(BF16)


def expert_forward(slot, x, w_gate, w_up, w_down):
    rows, width = x.shape
    feat = w_gate.shape[2]
    tile = rows // 4
    weight = pl.BlockSpec((None, width, feat), lambda i, s: (s[0], 0, 0))
    wide = pl.BlockSpec((tile, width), lambda i, s: (i, 0))
    thin = pl.BlockSpec((tile, feat), lambda i, s: (i, 0))
    return pl.pallas_call(
        forward_kernel,
        grid_spec=pltpu.PrefetchScalarGridSpec(
            num_scalar_prefetch=1,
            grid=(rows // tile,),
            in_specs=[wide, weight, weight, weight],
            out_specs=[wide, thin, thin, thin],
        ),
        out_shape=[
            jax.ShapeDtypeStruct((rows, width), BF16),
            jax.ShapeDtypeStruct((rows, feat), BF16),
            jax.ShapeDtypeStruct((rows, feat), F32),
            jax.ShapeDtypeStruct((rows, feat), F32),
        ],
        compiler_params=pltpu.CompilerParams(vmem_limit_bytes=VMEM_BYTES),
        cost_estimate=pl.CostEstimate(
            flops=6 * rows * width * feat,
            bytes_accessed=4 * rows * width + 6 * width * feat + 10 * rows * feat,
            transcendentals=rows * feat,
        ),
    )(slot, x, w_gate, w_up, w_down)


def expert_backward(slot, c, dgate, dup, w_gate, w_up, w_down):
    rows, width = c.shape
    feat = w_gate.shape[2]
    tile = rows // 4
    weight = pl.BlockSpec((None, width, feat), lambda i, s: (s[0], 0, 0))
    wide = pl.BlockSpec((tile, width), lambda i, s: (i, 0))
    thin = pl.BlockSpec((tile, feat), lambda i, s: (i, 0))
    return pl.pallas_call(
        backward_kernel,
        grid_spec=pltpu.PrefetchScalarGridSpec(
            num_scalar_prefetch=1,
            grid=(rows // tile,),
            in_specs=[wide, thin, thin, weight, weight, weight],
            out_specs=[wide, thin, thin],
        ),
        out_shape=[
            jax.ShapeDtypeStruct((rows, width), BF16),
            jax.ShapeDtypeStruct((rows, feat), BF16),
            jax.ShapeDtypeStruct((rows, feat), BF16),
        ],
        compiler_params=pltpu.CompilerParams(vmem_limit_bytes=VMEM_BYTES),
        cost_estimate=pl.CostEstimate(
            flops=6 * rows * width * feat,
            bytes_accessed=4 * rows * width + 6 * width * feat + 12 * rows * feat,
            transcendentals=0,
        ),
    )(slot, c, dgate, dup, w_gate, w_up, w_down)


def expert_grads(lhs, rights, parts):
    rows, width = lhs.shape
    feat = rights[0].shape[1]
    number = len(rights)
    cols = width // parts
    thin = pl.BlockSpec((rows, feat), lambda i: (0, 0))
    return pl.pallas_call(
        grads_kernel,
        grid=(parts,),
        in_specs=[pl.BlockSpec((rows, cols), lambda i: (0, i))] + [thin] * number,
        out_specs=pl.BlockSpec((1, number, cols, feat), lambda i: (i, 0, 0, 0)),
        out_shape=jax.ShapeDtypeStruct((parts, number, cols, feat), BF16),
        compiler_params=pltpu.CompilerParams(vmem_limit_bytes=VMEM_BYTES),
        cost_estimate=pl.CostEstimate(
            flops=2 * number * rows * width * feat,
            bytes_accessed=2 * rows * width + 2 * number * (width + rows) * feat,
            transcendentals=0,
        ),
    )(lhs, *rights)


def local(tokens, cotangent, expert_ids, combine_weights, w_gate, w_up, w_down, swap_flags):
    tok_rows, width = tokens.shape
    top_count = expert_ids.shape[1]
    per_device = w_gate.shape[0]
    groups = lax.axis_size("expert")
    parts = lax.axis_size("dp")
    half = groups // 2
    experts_all = groups * per_device
    capacity = tok_rows * top_count * 5 // (4 * experts_all) * parts
    total = groups * capacity
    mine = lax.axis_index("dp")
    slot = mine.astype(jnp.int32).reshape(1)

    info = jnp.concatenate([expert_ids.astype(F32), combine_weights], axis=1)
    info = lax.all_gather(info, "dp", tiled=True)
    tok_all = lax.all_gather(tokens, "dp", tiled=True)
    cot_all = lax.all_gather(cotangent, "dp", tiled=True)
    ids = info[:, :top_count].astype(jnp.int32)
    weights = info[:, top_count:]
    count = ids.shape[0]
    wanted = jnp.arange(groups, dtype=jnp.int32) * per_device + mine
    match = ids[:, :, None] == wanted[None, None, :]
    hit = jnp.any(match, axis=1)
    route_weight = jnp.sum(jnp.where(match, weights[:, :, None], 0.0), axis=1)
    below = (jnp.arange(count)[:, None] > jnp.arange(count)[None, :]).astype(BF16)
    rank = dot(below, hit.astype(BF16), ((1,), (0,))).astype(jnp.int32)
    place = jnp.where(hit, rank, -1).T
    picked = place[:, None, :] == jnp.arange(capacity, dtype=jnp.int32)[None, :, None]
    row_weight = jnp.sum(jnp.where(picked, route_weight.T[:, None, :], 0.0), axis=2).reshape(total, 1)
    pick = picked.astype(BF16).reshape(total, count)
    pick_weighted = (
        jnp.where(picked, route_weight.T[:, None, :], 0.0).astype(BF16).reshape(total, count)
    )

    def exchange(value):
        shape = (groups, capacity, width)
        return lax.all_to_all(
            value.reshape(shape), "expert", split_axis=0, concat_axis=0, tiled=True
        ).reshape(total, width)

    x = exchange(dot(pick, tok_all, ((1,), (0,))).astype(BF16))
    c = exchange((dot(pick, cot_all, ((1,), (0,))) * row_weight).astype(BF16))
    out, hidden, dgate, dup = expert_forward(slot, x, w_gate, w_up, w_down)
    out_back = exchange(out)

    def blocks(grads):
        return [
            lax.dynamic_index_in_dim(grads, mine ^ step, keepdims=False) for step in range(parts)
        ]

    def swap(block, step):
        return lax.ppermute(block, "dp", [(i, i ^ step) for i in range(parts)])

    down = blocks(expert_grads(c, [hidden], parts))
    dgate, *down = lax.optimization_barrier((dgate, *down))
    down = down[:1] + [swap(down[step], step) for step in range(1, parts)]
    term, gate_cot, up_cot = expert_backward(slot, c, dgate, dup, w_gate, w_up, w_down)
    both = blocks(expert_grads(x, [gate_cot, up_cot], parts))
    both[0], *moved = lax.optimization_barrier((both[0], *both[1:], *down[1:]))
    both, down = both[:1] + moved[: parts - 1], down[:1] + moved[parts - 1 :]
    both = both[:1] + [swap(both[step], step) for step in range(1, parts)]
    term, *ready = lax.optimization_barrier((term, *down, *both[:-1]))
    term_back = exchange(term)
    term_back, final = lax.optimization_barrier((term_back, both[-1]))
    down, both = ready[:parts], [*ready[parts:], final]
    received = [jnp.concatenate([b, d], axis=0) for b, d in zip(both, down)]

    mixed_part = dot(pick_weighted, out_back, ((0,), (0,))).astype(BF16)
    mixed = lax.psum_scatter(mixed_part, "dp", scatter_dimension=0, tiled=True)
    input_part = dot(pick, term_back, ((0,), (0,))).astype(BF16)
    input_grad = lax.psum_scatter(input_part, "dp", scatter_dimension=0, tiled=True)

    last = lax.select_n((per_device - 1) ^ mine, *received)
    pairs = [(i, (i + half) % groups) for i in range(groups)]
    peer = lax.ppermute(last, "expert", pairs)
    pair = lax.axis_index("expert") % half
    flag = jnp.sum(jnp.where(jnp.arange(half) == pair, swap_flags, 0)) == 1
    chosen = jnp.where(flag, peer, last)
    out_grads = []
    for m in range(3):
        whole = jnp.zeros((per_device,) + last.shape[1:], BF16)
        for step in range(parts):
            whole = lax.dynamic_update_index_in_dim(whole, received[step][m], mine ^ step, 0)
        out_grads.append(whole.at[per_device - 1].set(chosen[m]))
    return (mixed, input_grad, *out_grads)


MESH = pl.DeviceIdType.MESH
KERNEL_VMEM = 60 * 1024 * 1024
STRIPE = 512


def plane_kernel(
    cap,
    own, info, wg, wu, wd, flags,
    mixed, igrad, gg, gu, gd, everyone, first, second,
    infos, wgu, wdv, acc_in, acc_down, xs, cs, stage, part, picks, row_weights, peer,
    send_block, send_info, send_z, send_zinfo, recv_block, recv_info,
    local_sem, stage_sem, send_first, recv_first, send_second, recv_second, send_swap, recv_swap,
):
    parts, groups = everyone.shape[0], everyone.shape[1]
    toks, width = own.shape[1], own.shape[2]
    experts, _, feat = wg.shape
    top = info.shape[0] // 2
    cut = width // parts
    rows = experts * 2 * cap
    j = lax.axis_index("expert")
    z = lax.axis_index("dp")
    core = j % 2
    chip = j // 2
    across_x = (j // 4) * 4 + (1 - chip % 2) * 2 + core
    across_y = (1 - j // 4) * 4 + (chip % 2) * 2 + core
    mate = j + 1 - 2 * core
    near = across_x + core * (across_y - across_x)
    next_one = across_y + core * (across_x - across_y)
    far = (3 - chip) * 2 + core

    barrier = pltpu.get_barrier_semaphore()
    for other in (across_x, across_y, mate):
        pl.semaphore_signal(barrier, inc=1, device_id=(other, z), device_id_type=MESH)
    for step in range(1, parts):
        pl.semaphore_signal(
            barrier, inc=1, device_id=(j, (z + step) % parts), device_id_type=MESH
        )
    locals_ = [
        pltpu.make_async_copy(wg, wgu.at[:, :, pl.ds(0, feat)], local_sem.at[0]),
        pltpu.make_async_copy(wu, wgu.at[:, :, pl.ds(feat, feat)], local_sem.at[1]),
        pltpu.make_async_copy(wd, wdv, local_sem.at[2]),
        pltpu.make_async_copy(own, everyone.at[z, j], local_sem.at[3]),
    ]
    locals_[3].start()
    infos[z, j] = info[...]
    pl.semaphore_wait(barrier, 2 + parts)

    def remote(src, dst, send, recv, to, plane=None):
        return pltpu.make_async_remote_copy(
            src_ref=src, dst_ref=dst, send_sem=send, recv_sem=recv,
            device_id=(to, z if plane is None else plane), device_id_type=MESH,
        )

    def pass_on(k, kind, zc, block, to, source=None, source_info=None):
        return (
            remote(
                everyone.at[zc, block] if source is None else source,
                everyone.at[zc, block],
                send_block.at[k, kind], recv_block.at[zc, block], to,
            ),
            remote(
                infos.at[zc, block] if source_info is None else source_info,
                infos.at[zc, block],
                send_info.at[k, kind], recv_info.at[zc, block], to,
            ),
        )

    def along_z(k):
        to = (z + k) % parts
        return (
            remote(own, everyone.at[z, j], send_z.at[k], recv_block.at[z, j], j, to),
            remote(info, infos.at[z, j], send_zinfo.at[k], recv_info.at[z, j], j, to),
        )

    def start(pair):
        pair[0].start()
        pair[1].start()

    def arrived(zc, block):
        for copy in pass_on(0, 0, zc, block, mate):
            copy.wait_recv()

    start(pass_on(0, 0, z, j, near, own, info))
    start(pass_on(0, 1, z, j, next_one, own, info))
    start(along_z(1))
    start(pass_on(0, 3, z, j, mate, own, info))
    for copy in locals_[:3]:
        copy.start()
    acc_in[...] = jnp.zeros_like(acc_in)
    acc_down[...] = jnp.zeros_like(acc_down)
    for copy in locals_:
        copy.wait()

    def chip_at(i):
        return jnp.where(
            i == 0, chip, jnp.where(i == 1, near // 2, jnp.where(i == 2, next_one // 2, far // 2))
        )

    def bring(zc, i):
        return pltpu.make_async_copy(
            everyone.at[zc, pl.ds(2 * chip_at(i), 2)], stage.at[i % 2], stage_sem.at[i % 2]
        )

    def gather(zc, i):
        hits, weights = [], []
        at = chip_at(i)
        for s in range(experts):
            name = (experts * j + s).astype(F32)
            for b in range(2):
                table = infos[zc, 2 * at + b]
                match = table[:top] == name
                hits.append(jnp.sum(jnp.where(match, 1.0, 0.0), axis=0, keepdims=True))
                weights.append(jnp.sum(jnp.where(match, table[top:], 0.0), axis=0, keepdims=True))
        hit = jnp.concatenate(hits, axis=0)
        before = (
            lax.broadcasted_iota(jnp.int32, (toks, toks), 0)
            < lax.broadcasted_iota(jnp.int32, (toks, toks), 1)
        )
        rank = dot(hit.astype(BF16), jnp.where(before, 1.0, 0.0).astype(BF16), ((1,), (0,)))
        line = lax.broadcasted_iota(jnp.int32, (2 * cap, 2 * toks), 0).astype(F32)
        chosen, scales = [], []
        for s in range(experts):
            place = jnp.concatenate(
                [
                    jnp.where(hits[2 * s + b] > 0, rank[2 * s + b : 2 * s + b + 1] + cap * b, -1.0)
                    for b in range(2)
                ],
                axis=1,
            )
            weight = jnp.concatenate(weights[2 * s : 2 * s + 2], axis=1)
            same = line == place
            chosen.append(jnp.where(same, 1.0, 0.0).astype(BF16))
            scales.append(jnp.sum(jnp.where(same, weight, 0.0), axis=1, keepdims=True))
        pick = jnp.concatenate(chosen, axis=0)
        scale = jnp.concatenate(scales, axis=0)
        picks[i] = pick
        row_weights[i] = scale
        for n in range(width // STRIPE):
            cols = pl.ds(n * STRIPE, STRIPE)
            tok = stage[i % 2, :, 0, :, cols].reshape(2 * toks, STRIPE)
            xs[i, :, cols] = dot(pick, tok, ((1,), (0,))).astype(BF16)
            cot = stage[i % 2, :, 1, :, cols].reshape(2 * toks, STRIPE)
            cs[i, :, cols] = (dot(pick, cot, ((1,), (0,))) * scale).astype(BF16)

    def expert(k, s):
        mine = pl.ds(pl.multiple_of(s * 2 * cap, 16), 2 * cap)
        count = groups * cap
        x = xs[:, mine, :].reshape(count, width)
        both = dot(x, wgu[s], ((1,), (0,)))
        c = cs[:, mine, :].reshape(count, width)
        hidden_cot = dot(c, wdv[s], ((1,), (0,)))
        gate, up = both[:, :feat], both[:, feat:]
        sig = jax.nn.sigmoid(gate)
        silu = gate * sig
        hidden = (silu * up).astype(BF16)
        cots = jnp.concatenate(
            [
                (hidden_cot * up * sig * (1.0 + gate * (1.0 - sig))).astype(BF16),
                (hidden_cot * silu).astype(BF16),
            ],
            axis=1,
        )
        here = pl.ds(pl.multiple_of(z * cut, cut), cut)
        acc_in[s] += dot(xs[:, mine, here].reshape(count, cut), cots, ((0,), (0,)))
        acc_down[s] += dot(cs[:, mine, here].reshape(count, cut), hidden, ((0,), (0,)))

        @pl.when(k == 0)
        def _():
            scale = row_weights[:, mine, :].reshape(count, 1)
            for n in range(width // STRIPE):
                cols = pl.ds(n * STRIPE, STRIPE)
                out = dot(hidden, wdv[s, cols, :], ((1,), (1,))) * scale
                xs[:, mine, cols] = out.astype(BF16).reshape(groups // 2, 2 * cap, STRIPE)
                term = dot(cots, wgu[s, cols, :], ((1,), (1,)))
                cs[:, mine, cols] = term.astype(BF16).reshape(groups // 2, 2 * cap, STRIPE)

    def swaps():
        last = experts - 1
        return [
            remote(ref.at[last], peer.at[m], send_swap.at[m], recv_swap.at[m], across_y)
            for m, ref in enumerate((gg, gu, gd))
        ]

    def to_mate(i):
        there = (2 * i) % 3 + 3 * (i // 3)
        return remote(
            stage.at[i % 2, 1 - core], first.at[there], send_first.at[i], recv_first.at[there], mate
        )

    def from_mate(i):
        return remote(
            stage.at[i % 2, 1 - core], first.at[i], send_first.at[i], recv_first.at[i], mate
        )

    def combine(i, _):
        @pl.when(i >= 2)
        def _():
            to_mate(i - 2).wait_send()

        for n in range(width // STRIPE):
            cols = pl.ds(n * STRIPE, STRIPE)
            for a, ref in enumerate((xs, cs)):
                total = dot(picks[i], ref[i, :, cols], ((0,), (0,))).astype(BF16)
                stage[i % 2, :, a, :, cols] = total.reshape(2, toks, STRIPE)
        to_mate(i).start()
        part[i] = stage[i % 2, core]
        return 0

    def reduce_copy(which):
        source, to = ((3, near), (1, near), (2, next_one))[which]
        return remote(
            part.at[source], second.at[which], send_second.at[which],
            recv_second.at[which], to,
        )

    def fetch(ref, at, slot):
        copy = pltpu.make_async_copy(ref.at[at], stage.at[slot, 0], stage_sem.at[slot])
        copy.start()
        copy.wait()
        return stage[slot, 0]

    def add_mate():
        def one(i, _):
            from_mate(i).wait_recv()
            got = fetch(first, i, 0)
            part[i] = (part[i].astype(F32) + got.astype(F32)).astype(BF16)
            return 0

        lax.fori_loop(0, groups // 2, one, 0)
        reduce_copy(0).start()
        reduce_copy(1).start()

    def add_relay():
        reduce_copy(0).wait_recv()
        got = fetch(second, 0, 0)
        part[2] = (part[2].astype(F32) + got.astype(F32)).astype(BF16)
        reduce_copy(2).start()

    def chunk(k, _):
        zc = (z + parts - k) % parts
        arrived(zc, near)
        start(pass_on(k, 2, zc, near, next_one))
        start(pass_on(k, 4, zc, near, mate))
        arrived(zc, next_one)
        start(pass_on(k, 5, zc, next_one, mate))

        @pl.when(k < parts - 2)
        def _():
            start(along_z(k + 2))

        @pl.when(k < parts - 1)
        def _():
            zn = (z + parts - k - 1) % parts
            arrived(zn, j)
            start(pass_on(k + 1, 0, zn, j, near))
            start(pass_on(k + 1, 1, zn, j, next_one))
            start(pass_on(k + 1, 3, zn, j, mate))

        arrived(zc, mate)
        bring(zc, 0).start()

        def pair(i, _):
            @pl.when(i == 2)
            def _():
                arrived(zc, far)
                start(pass_on(k, 6, zc, far, mate))

            @pl.when(i < groups // 2 - 1)
            def _():
                arrived(zc, 2 * chip_at(i + 1) + 1 - core)
                bring(zc, i + 1).start()

            bring(zc, i).wait()
            gather(zc, i)
            return 0

        lax.fori_loop(0, groups // 2, pair, 0)

        def each(i, _):
            s = experts - 1 - i
            expert(k, s)

            @pl.when(k == parts - 1)
            def _():
                gg[s] = acc_in[s, :, :feat].astype(BF16)
                gu[s] = acc_in[s, :, feat:].astype(BF16)
                gd[s] = acc_down[s].astype(BF16)

                @pl.when(i == 0)
                def _():
                    for copy in swaps():
                        copy.start()

            return 0

        lax.fori_loop(0, experts, each, 0)

        @pl.when(k == 0)
        def _():
            lax.fori_loop(0, groups // 2, combine, 0)
            to_mate(2).wait_send()
            to_mate(3).wait_send()

        @pl.when(k == 1)
        def _():
            add_mate()

        @pl.when(k == 2)
        def _():
            add_relay()

        return 0

    lax.fori_loop(0, parts, chunk, 0)

    for which in (1, 2):
        reduce_copy(which).wait_recv()
    one, two = fetch(second, 1, 0).astype(F32), fetch(second, 2, 1).astype(F32)
    total = (part[0].astype(F32) + one + two).astype(BF16)
    mixed[...] = total[0]
    igrad[...] = total[1]
    for which in range(3):
        reduce_copy(which).wait_send()
    for copy in swaps():
        copy.wait_send()
    flag = flags[j % (groups // 2)]
    for m, (copy, ref) in enumerate(zip(swaps(), (gg, gu, gd))):
        copy.wait_recv()
        moved = jnp.full((cut, feat), flag) == 1
        ref[experts - 1] = jnp.where(
            moved, peer[m].astype(F32), ref[experts - 1].astype(F32)
        ).astype(BF16)
    for k in range(parts):
        for kind in range(7):
            for copy in pass_on(k, kind, z, j, mate):
                copy.wait_send()
        if k:
            for copy in along_z(k):
                copy.wait_send()


def local_plane(tokens, cotangent, expert_ids, combine_weights, w_gate, w_up, w_down, swap_flags):
    toks, width = tokens.shape
    top = expert_ids.shape[1]
    experts, _, feat = w_gate.shape
    groups = lax.axis_size("expert")
    parts = lax.axis_size("dp")
    cap = toks * top * 5 // (4 * groups * experts)
    cut = width // parts
    rows = experts * 2 * cap
    chips = groups // 2
    own = jnp.stack([tokens, cotangent])
    info = jnp.concatenate([expert_ids.astype(F32), combine_weights], axis=1).T
    hbm = pl.BlockSpec(memory_space=pltpu.HBM)
    vmem = pl.BlockSpec(memory_space=pltpu.VMEM)
    smem = pl.BlockSpec(memory_space=pltpu.SMEM)
    sem = pltpu.SemaphoreType.DMA
    grad = jax.ShapeDtypeStruct((experts, cut, feat), BF16)
    out = jax.ShapeDtypeStruct((toks, width), BF16)
    results = pl.pallas_call(
        functools.partial(plane_kernel, cap),
        in_specs=[hbm, vmem, hbm, hbm, hbm, smem],
        out_specs=[vmem] * 5 + [hbm] * 3,
        out_shape=[
            out, out, grad, grad, grad,
            jax.ShapeDtypeStruct((parts, groups, 2, toks, width), BF16),
            jax.ShapeDtypeStruct((chips, 2, toks, width), BF16),
            jax.ShapeDtypeStruct((3, 2, toks, width), BF16),
        ],
        scratch_shapes=[
            pltpu.VMEM((parts, groups, 2 * top, toks), F32),
            pltpu.VMEM((experts, width, 2 * feat), BF16),
            pltpu.VMEM((experts, width, feat), BF16),
            pltpu.VMEM((experts, cut, 2 * feat), F32),
            pltpu.VMEM((experts, cut, feat), F32),
            pltpu.VMEM((chips, rows, width), BF16),
            pltpu.VMEM((chips, rows, width), BF16),
            pltpu.VMEM((2, 2, 2, toks, width), BF16),
            pltpu.VMEM((chips, 2, toks, width), BF16),
            pltpu.VMEM((chips, rows, 2 * toks), BF16),
            pltpu.VMEM((chips, rows, 1), F32),
            pltpu.VMEM((3, cut, feat), BF16),
            sem((parts, 7)), sem((parts, 7)), sem((parts,)), sem((parts,)),
            sem((parts, groups)), sem((parts, groups)),
            sem((4,)), sem((2,)), sem((chips,)), sem((chips,)),
            sem((3,)), sem((3,)), sem((3,)), sem((3,)),
        ],
        compiler_params=pltpu.CompilerParams(
            collective_id=0, has_side_effects=True, vmem_limit_bytes=KERNEL_VMEM
        ),
        cost_estimate=pl.CostEstimate(
            flops=60_000_000_000, bytes_accessed=100_000_000, transcendentals=5120 * feat
        ),
    )(own, info, w_gate, w_up, w_down, swap_flags)
    return tuple(results[:5])


def solution(mesh):
    small = mesh.shape["expert"] == 8 and mesh.shape["dp"] == 4
    return jax.shard_map(
        local_plane if small else local,
        mesh=mesh,
        in_specs=(
            P(("expert", "dp"), None),
            P(("expert", "dp"), None),
            P(("expert", "dp"), None),
            P(("expert", "dp"), None),
            P("expert", None, None),
            P("expert", None, None),
            P("expert", None, None),
            P(),
        ),
        out_specs=(
            P(("expert", "dp"), None),
            P(("expert", "dp"), None),
            P("expert", "dp", None),
            P("expert", "dp", None),
            P("expert", "dp", None),
        ),
        check_vma=False,
    )
```

```python
import functools

import jax
import jax.numpy as jnp
from jax import lax
from jax.experimental import pallas as pl
from jax.experimental.pallas import tpu as pltpu
from jax.sharding import PartitionSpec as P

F32 = jnp.float32
BF16 = jnp.bfloat16
VMEM_BYTES = 56 * 1024 * 1024


def dot(a, b, dims):
    return lax.dot_general(a, b, (dims, ((), ())), preferred_element_type=F32)


def forward_kernel(slot_ref, x_ref, wg_ref, wu_ref, wd_ref, out_ref, hid_ref, dgate_ref, dup_ref):
    x = x_ref[...]
    gate = dot(x, wg_ref[...], ((1,), (0,)))
    up = dot(x, wu_ref[...], ((1,), (0,)))
    s = jax.nn.sigmoid(gate)
    silu = gate * s
    hidden = (silu * up).astype(BF16)
    hid_ref[...] = hidden
    dgate_ref[...] = up * s * (1.0 + gate * (1.0 - s))
    dup_ref[...] = silu
    out_ref[...] = dot(hidden, wd_ref[...], ((1,), (1,))).astype(BF16)


def backward_kernel(
    slot_ref, c_ref, dgate_ref, dup_ref, wg_ref, wu_ref, wd_ref, term_ref, gc_ref, uc_ref
):
    hidden_cot = dot(c_ref[...], wd_ref[...], ((1,), (0,)))
    gate_cot = (hidden_cot * dgate_ref[...]).astype(BF16)
    up_cot = (hidden_cot * dup_ref[...]).astype(BF16)
    gc_ref[...] = gate_cot
    uc_ref[...] = up_cot
    term_ref[...] = (
        dot(gate_cot, wg_ref[...], ((1,), (1,))) + dot(up_cot, wu_ref[...], ((1,), (1,)))
    ).astype(BF16)


def grads_kernel(lhs_ref, *refs):
    lhs = lhs_ref[...]
    out_ref = refs[-1]
    for k, right_ref in enumerate(refs[:-1]):
        out_ref[0, k] = dot(lhs, right_ref[...], ((0,), (0,))).astype(BF16)


def expert_forward(slot, x, w_gate, w_up, w_down):
    rows, width = x.shape
    feat = w_gate.shape[2]
    tile = rows // 4
    weight = pl.BlockSpec((None, width, feat), lambda i, s: (s[0], 0, 0))
    wide = pl.BlockSpec((tile, width), lambda i, s: (i, 0))
    thin = pl.BlockSpec((tile, feat), lambda i, s: (i, 0))
    return pl.pallas_call(
        forward_kernel,
        grid_spec=pltpu.PrefetchScalarGridSpec(
            num_scalar_prefetch=1,
            grid=(rows // tile,),
            in_specs=[wide, weight, weight, weight],
            out_specs=[wide, thin, thin, thin],
        ),
        out_shape=[
            jax.ShapeDtypeStruct((rows, width), BF16),
            jax.ShapeDtypeStruct((rows, feat), BF16),
            jax.ShapeDtypeStruct((rows, feat), F32),
            jax.ShapeDtypeStruct((rows, feat), F32),
        ],
        compiler_params=pltpu.CompilerParams(vmem_limit_bytes=VMEM_BYTES),
        cost_estimate=pl.CostEstimate(
            flops=6 * rows * width * feat,
            bytes_accessed=4 * rows * width + 6 * width * feat + 10 * rows * feat,
            transcendentals=rows * feat,
        ),
    )(slot, x, w_gate, w_up, w_down)


def expert_backward(slot, c, dgate, dup, w_gate, w_up, w_down):
    rows, width = c.shape
    feat = w_gate.shape[2]
    tile = rows // 4
    weight = pl.BlockSpec((None, width, feat), lambda i, s: (s[0], 0, 0))
    wide = pl.BlockSpec((tile, width), lambda i, s: (i, 0))
    thin = pl.BlockSpec((tile, feat), lambda i, s: (i, 0))
    return pl.pallas_call(
        backward_kernel,
        grid_spec=pltpu.PrefetchScalarGridSpec(
            num_scalar_prefetch=1,
            grid=(rows // tile,),
            in_specs=[wide, thin, thin, weight, weight, weight],
            out_specs=[wide, thin, thin],
        ),
        out_shape=[
            jax.ShapeDtypeStruct((rows, width), BF16),
            jax.ShapeDtypeStruct((rows, feat), BF16),
            jax.ShapeDtypeStruct((rows, feat), BF16),
        ],
        compiler_params=pltpu.CompilerParams(vmem_limit_bytes=VMEM_BYTES),
        cost_estimate=pl.CostEstimate(
            flops=6 * rows * width * feat,
            bytes_accessed=4 * rows * width + 6 * width * feat + 12 * rows * feat,
            transcendentals=0,
        ),
    )(slot, c, dgate, dup, w_gate, w_up, w_down)


def expert_grads(lhs, rights, parts):
    rows, width = lhs.shape
    feat = rights[0].shape[1]
    number = len(rights)
    cols = width // parts
    thin = pl.BlockSpec((rows, feat), lambda i: (0, 0))
    return pl.pallas_call(
        grads_kernel,
        grid=(parts,),
        in_specs=[pl.BlockSpec((rows, cols), lambda i: (0, i))] + [thin] * number,
        out_specs=pl.BlockSpec((1, number, cols, feat), lambda i: (i, 0, 0, 0)),
        out_shape=jax.ShapeDtypeStruct((parts, number, cols, feat), BF16),
        compiler_params=pltpu.CompilerParams(vmem_limit_bytes=VMEM_BYTES),
        cost_estimate=pl.CostEstimate(
            flops=2 * number * rows * width * feat,
            bytes_accessed=2 * rows * width + 2 * number * (width + rows) * feat,
            transcendentals=0,
        ),
    )(lhs, *rights)


def local(tokens, cotangent, expert_ids, combine_weights, w_gate, w_up, w_down, swap_flags):
    tok_rows, width = tokens.shape
    top_count = expert_ids.shape[1]
    per_device = w_gate.shape[0]
    groups = lax.axis_size("expert")
    parts = lax.axis_size("dp")
    half = groups // 2
    experts_all = groups * per_device
    capacity = tok_rows * top_count * 5 // (4 * experts_all) * parts
    total = groups * capacity
    mine = lax.axis_index("dp")
    slot = mine.astype(jnp.int32).reshape(1)

    info = jnp.concatenate([expert_ids.astype(F32), combine_weights], axis=1)
    info = lax.all_gather(info, "dp", tiled=True)
    tok_all = lax.all_gather(tokens, "dp", tiled=True)
    cot_all = lax.all_gather(cotangent, "dp", tiled=True)
    ids = info[:, :top_count].astype(jnp.int32)
    weights = info[:, top_count:]
    count = ids.shape[0]
    wanted = jnp.arange(groups, dtype=jnp.int32) * per_device + mine
    match = ids[:, :, None] == wanted[None, None, :]
    hit = jnp.any(match, axis=1)
    route_weight = jnp.sum(jnp.where(match, weights[:, :, None], 0.0), axis=1)
    below = (jnp.arange(count)[:, None] > jnp.arange(count)[None, :]).astype(BF16)
    rank = dot(below, hit.astype(BF16), ((1,), (0,))).astype(jnp.int32)
    place = jnp.where(hit, rank, -1).T
    picked = place[:, None, :] == jnp.arange(capacity, dtype=jnp.int32)[None, :, None]
    row_weight = jnp.sum(jnp.where(picked, route_weight.T[:, None, :], 0.0), axis=2).reshape(total, 1)
    pick = picked.astype(BF16).reshape(total, count)
    pick_weighted = (
        jnp.where(picked, route_weight.T[:, None, :], 0.0).astype(BF16).reshape(total, count)
    )

    def exchange(value):
        shape = (groups, capacity, width)
        return lax.all_to_all(
            value.reshape(shape), "expert", split_axis=0, concat_axis=0, tiled=True
        ).reshape(total, width)

    x = exchange(dot(pick, tok_all, ((1,), (0,))).astype(BF16))
    c = exchange((dot(pick, cot_all, ((1,), (0,))) * row_weight).astype(BF16))
    out, hidden, dgate, dup = expert_forward(slot, x, w_gate, w_up, w_down)
    out_back = exchange(out)

    def blocks(grads):
        return [
            lax.dynamic_index_in_dim(grads, mine ^ step, keepdims=False) for step in range(parts)
        ]

    def swap(block, step):
        return lax.ppermute(block, "dp", [(i, i ^ step) for i in range(parts)])

    down = blocks(expert_grads(c, [hidden], parts))
    dgate, *down = lax.optimization_barrier((dgate, *down))
    down = down[:1] + [swap(down[step], step) for step in range(1, parts)]
    term, gate_cot, up_cot = expert_backward(slot, c, dgate, dup, w_gate, w_up, w_down)
    both = blocks(expert_grads(x, [gate_cot, up_cot], parts))
    both[0], *moved = lax.optimization_barrier((both[0], *both[1:], *down[1:]))
    both, down = both[:1] + moved[: parts - 1], down[:1] + moved[parts - 1 :]
    both = both[:1] + [swap(both[step], step) for step in range(1, parts)]
    term, *ready = lax.optimization_barrier((term, *down, *both[:-1]))
    term_back = exchange(term)
    term_back, final = lax.optimization_barrier((term_back, both[-1]))
    down, both = ready[:parts], [*ready[parts:], final]
    received = [jnp.concatenate([b, d], axis=0) for b, d in zip(both, down)]

    mixed_part = dot(pick_weighted, out_back, ((0,), (0,))).astype(BF16)
    mixed = lax.psum_scatter(mixed_part, "dp", scatter_dimension=0, tiled=True)
    input_part = dot(pick, term_back, ((0,), (0,))).astype(BF16)
    input_grad = lax.psum_scatter(input_part, "dp", scatter_dimension=0, tiled=True)

    last = lax.select_n((per_device - 1) ^ mine, *received)
    pairs = [(i, (i + half) % groups) for i in range(groups)]
    peer = lax.ppermute(last, "expert", pairs)
    pair = lax.axis_index("expert") % half
    flag = jnp.sum(jnp.where(jnp.arange(half) == pair, swap_flags, 0)) == 1
    chosen = jnp.where(flag, peer, last)
    out_grads = []
    for m in range(3):
        whole = jnp.zeros((per_device,) + last.shape[1:], BF16)
        for step in range(parts):
            whole = lax.dynamic_update_index_in_dim(whole, received[step][m], mine ^ step, 0)
        out_grads.append(whole.at[per_device - 1].set(chosen[m]))
    return (mixed, input_grad, *out_grads)


MESH = pl.DeviceIdType.MESH
KERNEL_VMEM = 62 * 1024 * 1024
STRIPE = 512


def plane_kernel(
    cap,
    own, info, wg, wu, wd, flags,
    mixed, igrad, gg, gu, gd, everyone, first, second, acts,
    infos, wgu, wdv, acc_in, acc_down, xs, cs, stage, part, picks, row_weights, peer,
    send_block, send_info, send_z, send_zinfo, recv_block, recv_info, send_act, recv_act, act_sem,
    local_sem, stage_sem, send_first, recv_first, send_second, recv_second, send_swap, recv_swap,
):
    parts, groups = everyone.shape[0], everyone.shape[1]
    toks, width = own.shape[1], own.shape[2]
    experts, _, feat = wg.shape
    top = info.shape[0] // 2
    cut = width // parts
    rows = experts * 2 * cap
    j = lax.axis_index("expert")
    z = lax.axis_index("dp")
    core = j % 2
    chip = j // 2
    across_x = (j // 4) * 4 + (1 - chip % 2) * 2 + core
    across_y = (1 - j // 4) * 4 + (chip % 2) * 2 + core
    mate = j + 1 - 2 * core
    def near(k):
        swung = jnp.where(k == 2, 1, core)
        return across_x + swung * (across_y - across_x)

    def next_one(k):
        swung = jnp.where(k == 2, 1, core)
        return across_y + swung * (across_x - across_y)

    far = (3 - chip) * 2 + core
    half = z // 2
    outer = z + 1 - 2 * (z % 2)
    inner = 3 - z
    inside = (z + half) % 2

    here = pl.ds(pl.multiple_of(z * cut, cut), cut)

    def plane(k):
        return jnp.where(
            k == 0, z, jnp.where(k == 1, 2 - half, jnp.where(k == 2, 3 - 3 * half, outer))
        )

    barrier = pltpu.get_barrier_semaphore()
    for other in (across_x, across_y, mate):
        pl.semaphore_signal(barrier, inc=1, device_id=(other, z), device_id_type=MESH)
    pl.semaphore_signal(barrier, inc=1, device_id=(j, outer), device_id_type=MESH)

    @pl.when(inside == 1)
    def _():
        pl.semaphore_signal(barrier, inc=1, device_id=(j, inner), device_id_type=MESH)

    locals_ = [
        pltpu.make_async_copy(wg, wgu.at[:, :, pl.ds(0, feat)], local_sem.at[0]),
        pltpu.make_async_copy(wu, wgu.at[:, :, pl.ds(feat, feat)], local_sem.at[1]),
        pltpu.make_async_copy(wd, wdv, local_sem.at[2]),
        pltpu.make_async_copy(own, everyone.at[z, j], local_sem.at[3]),
    ]
    locals_[3].start()
    infos[z, j] = info[...]
    pl.semaphore_wait(barrier, 4 + inside)

    def remote(src, dst, send, recv, to, row=None):
        return pltpu.make_async_remote_copy(
            src_ref=src, dst_ref=dst, send_sem=send, recv_sem=recv,
            device_id=(to, z if row is None else row), device_id_type=MESH,
        )

    def pass_on(k, kind, zc, block, to, source=None, source_info=None):
        return (
            remote(
                everyone.at[zc, block] if source is None else source,
                everyone.at[zc, block],
                send_block.at[k, kind], recv_block.at[zc, block], to,
            ),
            remote(
                infos.at[zc, block] if source_info is None else source_info,
                infos.at[zc, block],
                send_info.at[k, kind], recv_info.at[zc, block], to,
            ),
        )

    def pass_slice(kind, block, to):
        ref = everyone.at[outer, block, :, :, here]
        return (
            remote(ref, ref, send_block.at[3, kind], recv_block.at[outer, block], to),
            remote(
                infos.at[outer, block], infos.at[outer, block],
                send_info.at[3, kind], recv_info.at[outer, block], to,
            ),
        )

    def send_acts(s):
        return [
            remote(
                ref.at[s, pl.ds(0, groups * cap)], acts.at[m, s],
                send_act.at[m, s], recv_act.at[m, s], j, outer,
            )
            for m, ref in enumerate((gg, gu, gd))
        ]

    def take_acts(s):
        return [
            pltpu.make_async_copy(
                acts.at[m, s], xs.at[s, :, pl.ds(cut + m * feat, feat)], act_sem.at[m, s]
            )
            for m in range(3)
        ]

    def along_z(slot, zc, to, source=None, source_info=None):
        return (
            remote(
                everyone.at[zc, j] if source is None else source,
                everyone.at[zc, j],
                send_z.at[slot], recv_block.at[zc, j], j, to,
            ),
            remote(
                infos.at[zc, j] if source_info is None else source_info,
                infos.at[zc, j],
                send_zinfo.at[slot], recv_info.at[zc, j], j, to,
            ),
        )

    def start(pair):
        pair[0].start()
        pair[1].start()

    def arrived(zc, block):
        for copy in pass_on(0, 0, zc, block, mate):
            copy.wait_recv()

    def arrived_slice(block):
        for copy in pass_slice(0, block, mate):
            copy.wait_recv()

    start(pass_on(0, 0, z, j, near(0), own, info))
    start(pass_on(0, 1, z, j, next_one(0), own, info))
    start(along_z(0, z, outer, own, info))

    @pl.when(inside == 1)
    def _():
        start(along_z(1, z, inner, own, info))

    start(pass_on(0, 3, z, j, mate, own, info))
    for copy in locals_[:3]:
        copy.start()
    acc_in[...] = jnp.zeros_like(acc_in)
    acc_down[...] = jnp.zeros_like(acc_down)
    for copy in locals_:
        copy.wait()

    def chip_at(k, i):
        return jnp.where(
            i == 0,
            chip,
            jnp.where(i == 1, near(k) // 2, jnp.where(i == 2, next_one(k) // 2, far // 2)),
        )

    def bring(k, i):
        return pltpu.make_async_copy(
            everyone.at[plane(k), pl.ds(2 * chip_at(k, i), 2)], stage.at[i % 2], stage_sem.at[i % 2]
        )

    def bring_slice(i):
        return pltpu.make_async_copy(
            everyone.at[outer, pl.ds(2 * chip_at(3, i), 2), :, :, here],
            stage.at[i % 2, :, :, :, pl.ds(0, cut)],
            stage_sem.at[i % 2],
        )

    def gather(zc, i, at, stripes):
        hits, weights = [], []
        for s in range(experts):
            name = (experts * j + s).astype(F32)
            for b in range(2):
                table = infos[zc, 2 * at + b]
                match = table[:top] == name
                hits.append(jnp.sum(jnp.where(match, 1.0, 0.0), axis=0, keepdims=True))
                weights.append(jnp.sum(jnp.where(match, table[top:], 0.0), axis=0, keepdims=True))
        hit = jnp.concatenate(hits, axis=0)
        before = (
            lax.broadcasted_iota(jnp.int32, (toks, toks), 0)
            < lax.broadcasted_iota(jnp.int32, (toks, toks), 1)
        )
        rank = dot(hit.astype(BF16), jnp.where(before, 1.0, 0.0).astype(BF16), ((1,), (0,)))
        line = lax.broadcasted_iota(jnp.int32, (2 * cap, 2 * toks), 0).astype(F32)
        chosen, scales = [], []
        for s in range(experts):
            place = jnp.concatenate(
                [
                    jnp.where(hits[2 * s + b] > 0, rank[2 * s + b : 2 * s + b + 1] + cap * b, -1.0)
                    for b in range(2)
                ],
                axis=1,
            )
            weight = jnp.concatenate(weights[2 * s : 2 * s + 2], axis=1)
            same = line == place
            chosen.append(jnp.where(same, 1.0, 0.0).astype(BF16))
            scales.append(jnp.sum(jnp.where(same, weight, 0.0), axis=1, keepdims=True))
        pick = jnp.concatenate(chosen, axis=0)
        scale = jnp.concatenate(scales, axis=0)
        picks[i] = pick
        row_weights[i] = scale
        for n in range(stripes):
            cols = pl.ds(n * STRIPE, STRIPE)
            tok = stage[i % 2, :, 0, :, cols].reshape(2 * toks, STRIPE)
            xs[i, :, cols] = dot(pick, tok, ((1,), (0,))).astype(BF16)
            cot = stage[i % 2, :, 1, :, cols].reshape(2 * toks, STRIPE)
            cs[i, :, cols] = (dot(pick, cot, ((1,), (0,))) * scale).astype(BF16)

    def expert(k, s):
        mine = pl.ds(pl.multiple_of(s * 2 * cap, 16), 2 * cap)
        count = groups * cap
        x = xs[:, mine, :].reshape(count, width)
        both = dot(x, wgu[s], ((1,), (0,)))
        c = cs[:, mine, :].reshape(count, width)
        hidden_cot = dot(c, wdv[s], ((1,), (0,)))
        gate, up = both[:, :feat], both[:, feat:]
        sig = jax.nn.sigmoid(gate)
        silu = gate * sig
        hidden = (silu * up).astype(BF16)
        cots = jnp.concatenate(
            [
                (hidden_cot * up * sig * (1.0 + gate * (1.0 - sig))).astype(BF16),
                (hidden_cot * silu).astype(BF16),
            ],
            axis=1,
        )
        acc_in[s] += dot(xs[:, mine, here].reshape(count, cut), cots, ((0,), (0,)))
        acc_down[s] += dot(cs[:, mine, here].reshape(count, cut), hidden, ((0,), (0,)))

        @pl.when(k == 0)
        def _():
            gg[s, pl.ds(0, count)] = cots[:, :feat]
            gu[s, pl.ds(0, count)] = cots[:, feat:]
            gd[s, pl.ds(0, count)] = hidden
            for copy in send_acts(s):
                copy.start()
            scale = row_weights[:, mine, :].reshape(count, 1)
            for n in range(width // STRIPE):
                cols = pl.ds(n * STRIPE, STRIPE)
                out = dot(hidden, wdv[s, cols, :], ((1,), (1,))) * scale
                xs[:, mine, cols] = out.astype(BF16).reshape(groups // 2, 2 * cap, STRIPE)
                term = dot(cots, wgu[s, cols, :], ((1,), (1,)))
                cs[:, mine, cols] = term.astype(BF16).reshape(groups // 2, 2 * cap, STRIPE)

    def swaps():
        last = experts - 1
        return [
            remote(ref.at[last], peer.at[m], send_swap.at[m], recv_swap.at[m], across_y)
            for m, ref in enumerate((gg, gu, gd))
        ]

    def to_mate(i):
        there = (2 * i) % 3 + 3 * (i // 3)
        return remote(
            stage.at[i % 2, 1 - core], first.at[there], send_first.at[i], recv_first.at[there], mate
        )

    def from_mate(i):
        return remote(
            stage.at[i % 2, 1 - core], first.at[i], send_first.at[i], recv_first.at[i], mate
        )

    def combine(i, _):
        @pl.when(i >= 2)
        def _():
            to_mate(i - 2).wait_send()

        for n in range(width // STRIPE):
            cols = pl.ds(n * STRIPE, STRIPE)
            for a, ref in enumerate((xs, cs)):
                total = dot(picks[i], ref[i, :, cols], ((0,), (0,))).astype(BF16)
                stage[i % 2, :, a, :, cols] = total.reshape(2, toks, STRIPE)
        to_mate(i).start()
        part[i] = stage[i % 2, core]
        return 0

    def reduce_copy(which):
        source, to = ((3, near(0)), (1, near(0)), (2, next_one(0)))[which]
        return remote(
            part.at[source], second.at[which], send_second.at[which],
            recv_second.at[which], to,
        )

    def fetch(ref, at, slot):
        copy = pltpu.make_async_copy(ref.at[at], stage.at[slot, 0], stage_sem.at[slot])
        copy.start()
        copy.wait()
        return stage[slot, 0]

    def add_mate():
        def one(i, _):
            from_mate(i).wait_recv()
            got = fetch(first, i, 0)
            part[i] = (part[i].astype(F32) + got.astype(F32)).astype(BF16)
            return 0

        lax.fori_loop(0, groups // 2, one, 0)
        reduce_copy(0).start()
        reduce_copy(1).start()

    def add_relay():
        reduce_copy(0).wait_recv()
        got = fetch(second, 0, 0)
        part[2] = (part[2].astype(F32) + got.astype(F32)).astype(BF16)
        reduce_copy(2).start()

    def column(k):
        zc = plane(k)

        @pl.when(inside == 0)
        def _():
            arrived(zc, j)

        start(pass_on(k, 0, zc, j, near(k)))
        start(pass_on(k, 1, zc, j, next_one(k)))
        start(pass_on(k, 3, zc, j, mate))

    def relay(k):
        zc = plane(k)
        arrived(zc, near(k))
        start(pass_on(k, 2, zc, near(k), next_one(k)))
        start(pass_on(k, 4, zc, near(k), mate))
        arrived(zc, next_one(k))
        start(pass_on(k, 5, zc, next_one(k), mate))

    def slice_relay():
        arrived_slice(near(3))
        start(pass_slice(2, near(3), next_one(3)))
        start(pass_slice(4, near(3), mate))
        arrived_slice(next_one(3))
        start(pass_slice(5, next_one(3), mate))

    relay(0)
    arrived(outer, j)

    @pl.when(inside == 1)
    def _():
        start(along_z(2, outer, inner))
        arrived(inner, j)
        start(along_z(3, inner, outer))

    start(pass_slice(0, j, near(3)))
    start(pass_slice(1, j, next_one(3)))
    start(pass_slice(3, j, mate))

    def slice_chunk():
        arrived_slice(mate)
        bring_slice(0).start()

        def pair(i, _):
            @pl.when(i < groups // 2 - 1)
            def _():
                arrived_slice(2 * chip_at(3, i + 1) + 1 - core)
                bring_slice(i + 1).start()

            bring_slice(i).wait()
            gather(outer, i, chip_at(3, i), cut // STRIPE)
            return 0

        lax.fori_loop(0, groups // 2, pair, 0)

        def take(s, _):
            for copy in send_acts(s):
                copy.wait_recv()
            for copy in take_acts(s):
                copy.start()
            return 0

        lax.fori_loop(0, experts, take, 0)

        def each(s, _):
            for copy in take_acts(s):
                copy.wait()
            mine = pl.ds(pl.multiple_of(s * 2 * cap, 16), 2 * cap)
            count = groups * cap
            x = xs[:, mine, pl.ds(0, cut)].reshape(count, cut)
            c = cs[:, mine, pl.ds(0, cut)].reshape(count, cut)
            acc_in[s] += dot(x, xs[s, :, pl.ds(cut, 2 * feat)], ((0,), (0,)))
            acc_down[s] += dot(c, xs[s, :, pl.ds(cut + 2 * feat, feat)], ((0,), (0,)))
            for copy in send_acts(s):
                copy.wait_send()
            return 0

        lax.fori_loop(0, experts, each, 0)

    def chunk(k, _):
        zc = plane(k)
        arrived(zc, mate)
        bring(k, 0).start()

        def pair(i, _):
            @pl.when(i == 2)
            def _():
                arrived(zc, far)
                start(pass_on(k, 6, zc, far, mate))

                @pl.when(k == 0)
                def _():
                    column(1)
                    slice_relay()

                    @pl.when(inside == 1)
                    def _():
                        arrived(plane(2), j)
                        start(along_z(4, plane(2), outer))

                @pl.when(k == 1)
                def _():
                    relay(2)
                    arrived_slice(far)
                    start(pass_slice(6, far, mate))

            @pl.when(i < groups // 2 - 1)
            def _():
                arrived(zc, 2 * chip_at(k, i + 1) + 1 - core)
                bring(k, i + 1).start()

            bring(k, i).wait()
            gather(zc, i, chip_at(k, i), width // STRIPE)
            return 0

        lax.fori_loop(0, groups // 2, pair, 0)

        @pl.when(k == 2)
        def _():
            add_relay()

        def each(i, _):
            s = experts - 1 - i
            expert(k, s)

            @pl.when((k == 0) & (i == 1))
            def _():
                relay(1)
                column(2)

            @pl.when(k == 2)
            def _():
                gg[s] = acc_in[s, :, :feat].astype(BF16)
                gu[s] = acc_in[s, :, feat:].astype(BF16)
                gd[s] = acc_down[s].astype(BF16)

                @pl.when(i == 0)
                def _():
                    for copy in swaps():
                        copy.start()

            return 0

        lax.fori_loop(0, experts, each, 0)

        @pl.when(k == 0)
        def _():
            lax.fori_loop(0, groups // 2, combine, 0)
            to_mate(2).wait_send()
            to_mate(3).wait_send()

        @pl.when(k == 1)
        def _():
            add_mate()
            slice_chunk()

        return 0

    lax.fori_loop(0, 3, chunk, 0)

    for which in (1, 2):
        reduce_copy(which).wait_recv()
    one, two = fetch(second, 1, 0).astype(F32), fetch(second, 2, 1).astype(F32)
    total = (part[0].astype(F32) + one + two).astype(BF16)
    mixed[...] = total[0]
    igrad[...] = total[1]
    for which in range(3):
        reduce_copy(which).wait_send()
    for copy in swaps():
        copy.wait_send()
    flag = flags[j % (groups // 2)]
    for m, (copy, ref) in enumerate(zip(swaps(), (gg, gu, gd))):
        copy.wait_recv()
        moved = jnp.full((cut, feat), flag) == 1
        ref[experts - 1] = jnp.where(
            moved, peer[m].astype(F32), ref[experts - 1].astype(F32)
        ).astype(BF16)
    for kind in range(7):
        for k in range(3):
            for copy in pass_on(k, kind, z, j, mate):
                copy.wait_send()
        for copy in pass_slice(kind, j, mate):
            copy.wait_send()
    for copy in along_z(0, z, outer):
        copy.wait_send()

    @pl.when(inside == 1)
    def _():
        for slot in range(1, 5):
            for copy in along_z(slot, z, outer):
                copy.wait_send()


def local_plane(tokens, cotangent, expert_ids, combine_weights, w_gate, w_up, w_down, swap_flags):
    toks, width = tokens.shape
    top = expert_ids.shape[1]
    experts, _, feat = w_gate.shape
    groups = lax.axis_size("expert")
    parts = lax.axis_size("dp")
    cap = toks * top * 5 // (4 * groups * experts)
    cut = width // parts
    rows = experts * 2 * cap
    chips = groups // 2
    own = jnp.stack([tokens, cotangent])
    info = jnp.concatenate([expert_ids.astype(F32), combine_weights], axis=1).T
    hbm = pl.BlockSpec(memory_space=pltpu.HBM)
    vmem = pl.BlockSpec(memory_space=pltpu.VMEM)
    smem = pl.BlockSpec(memory_space=pltpu.SMEM)
    sem = pltpu.SemaphoreType.DMA
    grad = jax.ShapeDtypeStruct((experts, cut, feat), BF16)
    out = jax.ShapeDtypeStruct((toks, width), BF16)
    results = pl.pallas_call(
        functools.partial(plane_kernel, cap),
        in_specs=[hbm, vmem, hbm, hbm, hbm, smem],
        out_specs=[vmem] * 5 + [hbm] * 4,
        out_shape=[
            out, out, grad, grad, grad,
            jax.ShapeDtypeStruct((parts, groups, 2, toks, width), BF16),
            jax.ShapeDtypeStruct((chips, 2, toks, width), BF16),
            jax.ShapeDtypeStruct((3, 2, toks, width), BF16),
            jax.ShapeDtypeStruct((3, experts, groups * cap, feat), BF16),
        ],
        scratch_shapes=[
            pltpu.VMEM((parts, groups, 2 * top, toks), F32),
            pltpu.VMEM((experts, width, 2 * feat), BF16),
            pltpu.VMEM((experts, width, feat), BF16),
            pltpu.VMEM((experts, cut, 2 * feat), F32),
            pltpu.VMEM((experts, cut, feat), F32),
            pltpu.VMEM((chips, rows, width), BF16),
            pltpu.VMEM((chips, rows, width), BF16),
            pltpu.VMEM((2, 2, 2, toks, width), BF16),
            pltpu.VMEM((chips, 2, toks, width), BF16),
            pltpu.VMEM((chips, rows, 2 * toks), BF16),
            pltpu.VMEM((chips, rows, 1), F32),
            pltpu.VMEM((3, cut, feat), BF16),
            sem((parts, 7)), sem((parts, 7)), sem((5,)), sem((5,)),
            sem((parts, groups)), sem((parts, groups)),
            sem((3, experts)), sem((3, experts)), sem((3, experts)),
            sem((4,)), sem((2,)), sem((chips,)), sem((chips,)),
            sem((3,)), sem((3,)), sem((3,)), sem((3,)),
        ],
        compiler_params=pltpu.CompilerParams(
            collective_id=0, has_side_effects=True, vmem_limit_bytes=KERNEL_VMEM
        ),
        cost_estimate=pl.CostEstimate(
            flops=60_000_000_000, bytes_accessed=100_000_000, transcendentals=5120 * feat
        ),
    )(own, info, w_gate, w_up, w_down, swap_flags)
    return tuple(results[:5])


def solution(mesh):
    small = mesh.shape["expert"] == 8 and mesh.shape["dp"] == 4
    return jax.shard_map(
        local_plane if small else local,
        mesh=mesh,
        in_specs=(
            P(("expert", "dp"), None),
            P(("expert", "dp"), None),
            P(("expert", "dp"), None),
            P(("expert", "dp"), None),
            P("expert", None, None),
            P("expert", None, None),
            P("expert", None, None),
            P(),
        ),
        out_specs=(
            P(("expert", "dp"), None),
            P(("expert", "dp"), None),
            P("expert", "dp", None),
            P("expert", "dp", None),
            P("expert", "dp", None),
        ),
        check_vma=False,
    )
```

```python
import functools

import jax
import jax.numpy as jnp
from jax import lax
from jax.experimental import pallas as pl
from jax.experimental.pallas import tpu as pltpu
from jax.sharding import PartitionSpec as P

F32 = jnp.float32
BF16 = jnp.bfloat16
VMEM_BYTES = 56 * 1024 * 1024


def dot(a, b, dims):
    return lax.dot_general(a, b, (dims, ((), ())), preferred_element_type=F32)


def forward_kernel(slot_ref, x_ref, wg_ref, wu_ref, wd_ref, out_ref, hid_ref, dgate_ref, dup_ref):
    x = x_ref[...]
    gate = dot(x, wg_ref[...], ((1,), (0,)))
    up = dot(x, wu_ref[...], ((1,), (0,)))
    s = jax.nn.sigmoid(gate)
    silu = gate * s
    hidden = (silu * up).astype(BF16)
    hid_ref[...] = hidden
    dgate_ref[...] = up * s * (1.0 + gate * (1.0 - s))
    dup_ref[...] = silu
    out_ref[...] = dot(hidden, wd_ref[...], ((1,), (1,))).astype(BF16)


def backward_kernel(
    slot_ref, c_ref, dgate_ref, dup_ref, wg_ref, wu_ref, wd_ref, term_ref, gc_ref, uc_ref
):
    hidden_cot = dot(c_ref[...], wd_ref[...], ((1,), (0,)))
    gate_cot = (hidden_cot * dgate_ref[...]).astype(BF16)
    up_cot = (hidden_cot * dup_ref[...]).astype(BF16)
    gc_ref[...] = gate_cot
    uc_ref[...] = up_cot
    term_ref[...] = (
        dot(gate_cot, wg_ref[...], ((1,), (1,))) + dot(up_cot, wu_ref[...], ((1,), (1,)))
    ).astype(BF16)


def grads_kernel(lhs_ref, *refs):
    lhs = lhs_ref[...]
    out_ref = refs[-1]
    for k, right_ref in enumerate(refs[:-1]):
        out_ref[0, k] = dot(lhs, right_ref[...], ((0,), (0,))).astype(BF16)


def expert_forward(slot, x, w_gate, w_up, w_down):
    rows, width = x.shape
    feat = w_gate.shape[2]
    tile = rows // 4
    weight = pl.BlockSpec((None, width, feat), lambda i, s: (s[0], 0, 0))
    wide = pl.BlockSpec((tile, width), lambda i, s: (i, 0))
    thin = pl.BlockSpec((tile, feat), lambda i, s: (i, 0))
    return pl.pallas_call(
        forward_kernel,
        grid_spec=pltpu.PrefetchScalarGridSpec(
            num_scalar_prefetch=1,
            grid=(rows // tile,),
            in_specs=[wide, weight, weight, weight],
            out_specs=[wide, thin, thin, thin],
        ),
        out_shape=[
            jax.ShapeDtypeStruct((rows, width), BF16),
            jax.ShapeDtypeStruct((rows, feat), BF16),
            jax.ShapeDtypeStruct((rows, feat), F32),
            jax.ShapeDtypeStruct((rows, feat), F32),
        ],
        compiler_params=pltpu.CompilerParams(vmem_limit_bytes=VMEM_BYTES),
        cost_estimate=pl.CostEstimate(
            flops=6 * rows * width * feat,
            bytes_accessed=4 * rows * width + 6 * width * feat + 10 * rows * feat,
            transcendentals=rows * feat,
        ),
    )(slot, x, w_gate, w_up, w_down)


def expert_backward(slot, c, dgate, dup, w_gate, w_up, w_down):
    rows, width = c.shape
    feat = w_gate.shape[2]
    tile = rows // 4
    weight = pl.BlockSpec((None, width, feat), lambda i, s: (s[0], 0, 0))
    wide = pl.BlockSpec((tile, width), lambda i, s: (i, 0))
    thin = pl.BlockSpec((tile, feat), lambda i, s: (i, 0))
    return pl.pallas_call(
        backward_kernel,
        grid_spec=pltpu.PrefetchScalarGridSpec(
            num_scalar_prefetch=1,
            grid=(rows // tile,),
            in_specs=[wide, thin, thin, weight, weight, weight],
            out_specs=[wide, thin, thin],
        ),
        out_shape=[
            jax.ShapeDtypeStruct((rows, width), BF16),
            jax.ShapeDtypeStruct((rows, feat), BF16),
            jax.ShapeDtypeStruct((rows, feat), BF16),
        ],
        compiler_params=pltpu.CompilerParams(vmem_limit_bytes=VMEM_BYTES),
        cost_estimate=pl.CostEstimate(
            flops=6 * rows * width * feat,
            bytes_accessed=4 * rows * width + 6 * width * feat + 12 * rows * feat,
            transcendentals=0,
        ),
    )(slot, c, dgate, dup, w_gate, w_up, w_down)


def expert_grads(lhs, rights, parts):
    rows, width = lhs.shape
    feat = rights[0].shape[1]
    number = len(rights)
    cols = width // parts
    thin = pl.BlockSpec((rows, feat), lambda i: (0, 0))
    return pl.pallas_call(
        grads_kernel,
        grid=(parts,),
        in_specs=[pl.BlockSpec((rows, cols), lambda i: (0, i))] + [thin] * number,
        out_specs=pl.BlockSpec((1, number, cols, feat), lambda i: (i, 0, 0, 0)),
        out_shape=jax.ShapeDtypeStruct((parts, number, cols, feat), BF16),
        compiler_params=pltpu.CompilerParams(vmem_limit_bytes=VMEM_BYTES),
        cost_estimate=pl.CostEstimate(
            flops=2 * number * rows * width * feat,
            bytes_accessed=2 * rows * width + 2 * number * (width + rows) * feat,
            transcendentals=0,
        ),
    )(lhs, *rights)


def local(tokens, cotangent, expert_ids, combine_weights, w_gate, w_up, w_down, swap_flags):
    tok_rows, width = tokens.shape
    top_count = expert_ids.shape[1]
    per_device = w_gate.shape[0]
    groups = lax.axis_size("expert")
    parts = lax.axis_size("dp")
    half = groups // 2
    experts_all = groups * per_device
    capacity = tok_rows * top_count * 5 // (4 * experts_all) * parts
    total = groups * capacity
    mine = lax.axis_index("dp")
    slot = mine.astype(jnp.int32).reshape(1)

    info = jnp.concatenate([expert_ids.astype(F32), combine_weights], axis=1)
    info = lax.all_gather(info, "dp", tiled=True)
    tok_all = lax.all_gather(tokens, "dp", tiled=True)
    cot_all = lax.all_gather(cotangent, "dp", tiled=True)
    ids = info[:, :top_count].astype(jnp.int32)
    weights = info[:, top_count:]
    count = ids.shape[0]
    wanted = jnp.arange(groups, dtype=jnp.int32) * per_device + mine
    match = ids[:, :, None] == wanted[None, None, :]
    hit = jnp.any(match, axis=1)
    route_weight = jnp.sum(jnp.where(match, weights[:, :, None], 0.0), axis=1)
    below = (jnp.arange(count)[:, None] > jnp.arange(count)[None, :]).astype(BF16)
    rank = dot(below, hit.astype(BF16), ((1,), (0,))).astype(jnp.int32)
    place = jnp.where(hit, rank, -1).T
    picked = place[:, None, :] == jnp.arange(capacity, dtype=jnp.int32)[None, :, None]
    row_weight = jnp.sum(jnp.where(picked, route_weight.T[:, None, :], 0.0), axis=2).reshape(total, 1)
    pick = picked.astype(BF16).reshape(total, count)
    pick_weighted = (
        jnp.where(picked, route_weight.T[:, None, :], 0.0).astype(BF16).reshape(total, count)
    )

    def exchange(value):
        shape = (groups, capacity, width)
        return lax.all_to_all(
            value.reshape(shape), "expert", split_axis=0, concat_axis=0, tiled=True
        ).reshape(total, width)

    x = exchange(dot(pick, tok_all, ((1,), (0,))).astype(BF16))
    c = exchange((dot(pick, cot_all, ((1,), (0,))) * row_weight).astype(BF16))
    out, hidden, dgate, dup = expert_forward(slot, x, w_gate, w_up, w_down)
    out_back = exchange(out)

    def blocks(grads):
        return [
            lax.dynamic_index_in_dim(grads, mine ^ step, keepdims=False) for step in range(parts)
        ]

    def swap(block, step):
        return lax.ppermute(block, "dp", [(i, i ^ step) for i in range(parts)])

    down = blocks(expert_grads(c, [hidden], parts))
    dgate, *down = lax.optimization_barrier((dgate, *down))
    down = down[:1] + [swap(down[step], step) for step in range(1, parts)]
    term, gate_cot, up_cot = expert_backward(slot, c, dgate, dup, w_gate, w_up, w_down)
    both = blocks(expert_grads(x, [gate_cot, up_cot], parts))
    both[0], *moved = lax.optimization_barrier((both[0], *both[1:], *down[1:]))
    both, down = both[:1] + moved[: parts - 1], down[:1] + moved[parts - 1 :]
    both = both[:1] + [swap(both[step], step) for step in range(1, parts)]
    term, *ready = lax.optimization_barrier((term, *down, *both[:-1]))
    term_back = exchange(term)
    term_back, final = lax.optimization_barrier((term_back, both[-1]))
    down, both = ready[:parts], [*ready[parts:], final]
    received = [jnp.concatenate([b, d], axis=0) for b, d in zip(both, down)]

    mixed_part = dot(pick_weighted, out_back, ((0,), (0,))).astype(BF16)
    mixed = lax.psum_scatter(mixed_part, "dp", scatter_dimension=0, tiled=True)
    input_part = dot(pick, term_back, ((0,), (0,))).astype(BF16)
    input_grad = lax.psum_scatter(input_part, "dp", scatter_dimension=0, tiled=True)

    last = lax.select_n((per_device - 1) ^ mine, *received)
    pairs = [(i, (i + half) % groups) for i in range(groups)]
    peer = lax.ppermute(last, "expert", pairs)
    pair = lax.axis_index("expert") % half
    flag = jnp.sum(jnp.where(jnp.arange(half) == pair, swap_flags, 0)) == 1
    chosen = jnp.where(flag, peer, last)
    out_grads = []
    for m in range(3):
        whole = jnp.zeros((per_device,) + last.shape[1:], BF16)
        for step in range(parts):
            whole = lax.dynamic_update_index_in_dim(whole, received[step][m], mine ^ step, 0)
        out_grads.append(whole.at[per_device - 1].set(chosen[m]))
    return (mixed, input_grad, *out_grads)


MESH = pl.DeviceIdType.MESH
KERNEL_VMEM = 62 * 1024 * 1024
STRIPE = 512
LATE = True


def plane_kernel(
    cap,
    own, info, wg, wu, wd, flags,
    mixed, igrad, gg, gu, gd, everyone, first, second, acts,
    infos, wgu, wdv, acc_in, acc_down, xs, cs, stage, part, picks, row_weights, peer,
    send_block, send_info, send_z, send_zinfo, recv_column, recv_block, recv_info, send_act, recv_act, act_sem,
    local_sem, stage_sem, send_first, recv_first, send_second, recv_second, send_swap, recv_swap,
):
    parts, groups = everyone.shape[0], everyone.shape[1]
    toks, width = own.shape[1], own.shape[2]
    experts, _, feat = wg.shape
    top = info.shape[0] // 2
    cut = width // parts
    rows = experts * 2 * cap
    j = lax.axis_index("expert")
    z = lax.axis_index("dp")
    core = j % 2
    chip = j // 2
    across_x = (j // 4) * 4 + (1 - chip % 2) * 2 + core
    across_y = (1 - j // 4) * 4 + (chip % 2) * 2 + core
    mate = j + 1 - 2 * core
    def near(k):
        swung = jnp.where(k == 2, 1, core)
        return across_x + swung * (across_y - across_x)

    def next_one(k):
        swung = jnp.where(k == 2, 1, core)
        return across_y + swung * (across_x - across_y)

    far = (3 - chip) * 2 + core
    half = z // 2
    outer = z + 1 - 2 * (z % 2)
    inner = 3 - z
    inside = (z + half) % 2

    here = pl.ds(pl.multiple_of(z * cut, cut), cut)

    def plane(k):
        return jnp.where(
            k == 0, z, jnp.where(k == 1, 2 - half, jnp.where(k == 2, 3 - 3 * half, outer))
        )

    barrier = pltpu.get_barrier_semaphore()
    for other in (across_x, across_y, mate):
        pl.semaphore_signal(barrier, inc=1, device_id=(other, z), device_id_type=MESH)
    pl.semaphore_signal(barrier, inc=1, device_id=(j, outer), device_id_type=MESH)

    @pl.when(inside == 1)
    def _():
        pl.semaphore_signal(barrier, inc=1, device_id=(j, inner), device_id_type=MESH)

    locals_ = [
        pltpu.make_async_copy(wg, wgu.at[:, :, pl.ds(0, feat)], local_sem.at[0]),
        pltpu.make_async_copy(wu, wgu.at[:, :, pl.ds(feat, feat)], local_sem.at[1]),
        pltpu.make_async_copy(wd, wdv, local_sem.at[2]),
        pltpu.make_async_copy(own, stage.at[0, 0], local_sem.at[3]),
        pltpu.make_async_copy(stage.at[0, 0], everyone.at[z, j], local_sem.at[4]),
    ]
    locals_[3].start()
    infos[z, j] = info[...]
    pl.semaphore_wait(barrier, 4 + inside)

    def remote(src, dst, send, recv, to, row=None):
        return pltpu.make_async_remote_copy(
            src_ref=src, dst_ref=dst, send_sem=send, recv_sem=recv,
            device_id=(to, z if row is None else row), device_id_type=MESH,
        )

    def pass_on(k, kind, zc, block, to, source=None, source_info=None):
        return (
            remote(
                everyone.at[zc, block] if source is None else source,
                everyone.at[zc, block],
                send_block.at[k, kind], recv_block.at[zc, block], to,
            ),
            remote(
                infos.at[zc, block] if source_info is None else source_info,
                infos.at[zc, block],
                send_info.at[k, kind], recv_info.at[zc, block], to,
            ),
        )

    def pass_slice(kind, block, to):
        ref = everyone.at[outer, block, :, :, here]
        return (
            remote(ref, ref, send_block.at[3, kind], recv_block.at[outer, block], to),
            remote(
                infos.at[outer, block], infos.at[outer, block],
                send_info.at[3, kind], recv_info.at[outer, block], to,
            ),
        )

    def send_acts(s):
        return [
            remote(
                ref.at[s, pl.ds(0, groups * cap)], acts.at[m, s],
                send_act.at[m, s], recv_act.at[m, s], j, outer,
            )
            for m, ref in enumerate((gg, gu, gd))
        ]

    def take_acts(s):
        return [
            pltpu.make_async_copy(
                acts.at[m, s], xs.at[s, :, pl.ds(cut + m * feat, feat)], act_sem.at[m, s]
            )
            for m in range(3)
        ]

    def along_z(slot, zc, to, h, source=None):
        return remote(
            everyone.at[zc, j, h] if source is None else source.at[h],
            everyone.at[zc, j, h],
            send_z.at[slot, h], recv_column.at[zc, h], j, to,
        )

    def info_z(slot, zc, to, source=None):
        return remote(
            infos.at[zc, j] if source is None else source,
            infos.at[zc, j],
            send_zinfo.at[slot], recv_info.at[zc, j], j, to,
        )

    def slice_z(zc, source=None):
        there = pl.ds(pl.multiple_of((z + outer - zc) * cut, cut), cut)
        return remote(
            everyone.at[zc, j, :, :, there] if source is None else source.at[:, :, there],
            everyone.at[zc, j, :, :, there],
            send_z.at[0, 0], recv_column.at[zc, 0], j, outer,
        )

    def column_arrived(zc):
        for h in range(2):
            along_z(0, zc, outer, h).wait_recv()
        info_z(0, zc, outer).wait_recv()

    def forward(slot, zc, to):
        info_z(0, zc, outer).wait_recv()
        info_z(slot, zc, to).start()

    def start(pair):
        pair[0].start()
        pair[1].start()

    def arrived(zc, block):
        for copy in pass_on(0, 0, zc, block, mate):
            copy.wait_recv()

    def arrived_slice(block):
        for copy in pass_slice(0, block, mate):
            copy.wait_recv()

    start(pass_on(0, 0, z, j, near(0), own, info))
    start(pass_on(0, 1, z, j, next_one(0), own, info))
    info_z(0, z, outer, info).start()

    @pl.when(inside == 0)
    def _():
        for h in range(2):
            along_z(0, z, outer, h, own).start()

    @pl.when(inside == 1)
    def _():
        slice_z(z, own).start()
        info_z(1, z, inner, info).start()
        for h in range(2):
            along_z(1, z, inner, h, own).start()

    start(pass_on(0, 3, z, j, mate, own, info))
    locals_[3].wait()
    locals_[4].start()
    for copy in locals_[:3]:
        copy.start()
    acc_in[...] = jnp.zeros_like(acc_in)
    acc_down[...] = jnp.zeros_like(acc_down)
    locals_[4].wait()

    def chip_at(k, i):
        return jnp.where(
            i == 0,
            chip,
            jnp.where(i == 1, near(k) // 2, jnp.where(i == 2, next_one(k) // 2, far // 2)),
        )

    def bring(k, i):
        return pltpu.make_async_copy(
            everyone.at[plane(k), pl.ds(2 * chip_at(k, i), 2)], stage.at[i % 2], stage_sem.at[i % 2]
        )

    def bring_slice(i):
        return pltpu.make_async_copy(
            everyone.at[outer, pl.ds(2 * chip_at(3, i), 2), :, :, here],
            stage.at[i % 2, :, :, :, pl.ds(0, cut)],
            stage_sem.at[i % 2],
        )

    def gather(zc, i, at, stripes):
        hits, weights = [], []
        for s in range(experts):
            name = (experts * j + s).astype(F32)
            for b in range(2):
                table = infos[zc, 2 * at + b]
                match = table[:top] == name
                hits.append(jnp.sum(jnp.where(match, 1.0, 0.0), axis=0, keepdims=True))
                weights.append(jnp.sum(jnp.where(match, table[top:], 0.0), axis=0, keepdims=True))
        hit = jnp.concatenate(hits, axis=0)
        before = (
            lax.broadcasted_iota(jnp.int32, (toks, toks), 0)
            < lax.broadcasted_iota(jnp.int32, (toks, toks), 1)
        )
        rank = dot(hit.astype(BF16), jnp.where(before, 1.0, 0.0).astype(BF16), ((1,), (0,)))
        line = lax.broadcasted_iota(jnp.int32, (2 * cap, 2 * toks), 0).astype(F32)
        chosen, scales = [], []
        for s in range(experts):
            place = jnp.concatenate(
                [
                    jnp.where(hits[2 * s + b] > 0, rank[2 * s + b : 2 * s + b + 1] + cap * b, -1.0)
                    for b in range(2)
                ],
                axis=1,
            )
            weight = jnp.concatenate(weights[2 * s : 2 * s + 2], axis=1)
            same = line == place
            chosen.append(jnp.where(same, 1.0, 0.0).astype(BF16))
            scales.append(jnp.sum(jnp.where(same, weight, 0.0), axis=1, keepdims=True))
        pick = jnp.concatenate(chosen, axis=0)
        scale = jnp.concatenate(scales, axis=0)
        picks[i] = pick
        row_weights[i] = scale
        for n in range(stripes):
            cols = pl.ds(n * STRIPE, STRIPE)
            tok = stage[i % 2, :, 0, :, cols].reshape(2 * toks, STRIPE)
            xs[i, :, cols] = dot(pick, tok, ((1,), (0,))).astype(BF16)
            cot = stage[i % 2, :, 1, :, cols].reshape(2 * toks, STRIPE)
            cs[i, :, cols] = (dot(pick, cot, ((1,), (0,))) * scale).astype(BF16)

    def expert(k, s):
        mine = pl.ds(pl.multiple_of(s * 2 * cap, 16), 2 * cap)
        count = groups * cap
        x = xs[:, mine, :].reshape(count, width)
        both = dot(x, wgu[s], ((1,), (0,)))
        c = cs[:, mine, :].reshape(count, width)
        hidden_cot = dot(c, wdv[s], ((1,), (0,)))
        gate, up = both[:, :feat], both[:, feat:]
        sig = jax.nn.sigmoid(gate)
        silu = gate * sig
        hidden = (silu * up).astype(BF16)
        cots = jnp.concatenate(
            [
                (hidden_cot * up * sig * (1.0 + gate * (1.0 - sig))).astype(BF16),
                (hidden_cot * silu).astype(BF16),
            ],
            axis=1,
        )
        acc_in[s] += dot(xs[:, mine, here].reshape(count, cut), cots, ((0,), (0,)))
        acc_down[s] += dot(cs[:, mine, here].reshape(count, cut), hidden, ((0,), (0,)))

        @pl.when(k == 0)
        def _():
            gg[s, pl.ds(0, count)] = cots[:, :feat]
            gu[s, pl.ds(0, count)] = cots[:, feat:]
            gd[s, pl.ds(0, count)] = hidden
            for copy in send_acts(s):
                copy.start()
            scale = row_weights[:, mine, :].reshape(count, 1)
            for n in range(width // STRIPE):
                cols = pl.ds(n * STRIPE, STRIPE)
                out = dot(hidden, wdv[s, cols, :], ((1,), (1,))) * scale
                xs[:, mine, cols] = out.astype(BF16).reshape(groups // 2, 2 * cap, STRIPE)
                term = dot(cots, wgu[s, cols, :], ((1,), (1,)))
                cs[:, mine, cols] = term.astype(BF16).reshape(groups // 2, 2 * cap, STRIPE)

    def swaps():
        last = experts - 1
        return [
            remote(ref.at[last], peer.at[m], send_swap.at[m], recv_swap.at[m], across_y)
            for m, ref in enumerate((gg, gu, gd))
        ]

    def to_mate(i):
        there = (2 * i) % 3 + 3 * (i // 3)
        return remote(
            stage.at[i % 2, 1 - core], first.at[there], send_first.at[i], recv_first.at[there], mate
        )

    def from_mate(i):
        return remote(
            stage.at[i % 2, 1 - core], first.at[i], send_first.at[i], recv_first.at[i], mate
        )

    def combine(i, _):
        @pl.when(i >= 2)
        def _():
            to_mate(i - 2).wait_send()

        for n in range(width // STRIPE):
            cols = pl.ds(n * STRIPE, STRIPE)
            for a, ref in enumerate((xs, cs)):
                total = dot(picks[i], ref[i, :, cols], ((0,), (0,))).astype(BF16)
                stage[i % 2, :, a, :, cols] = total.reshape(2, toks, STRIPE)
        to_mate(i).start()
        part[i] = stage[i % 2, core]
        return 0

    def reduce_copy(which):
        source, to = ((3, near(0)), (1, near(0)), (2, next_one(0)))[which]
        return remote(
            part.at[source], second.at[which], send_second.at[which],
            recv_second.at[which], to,
        )

    def fetch(ref, at, slot):
        copy = pltpu.make_async_copy(ref.at[at], stage.at[slot, 0], stage_sem.at[slot])
        copy.start()
        copy.wait()
        return stage[slot, 0]

    def add_mate():
        def one(i, _):
            from_mate(i).wait_recv()
            got = fetch(first, i, 0)
            part[i] = (part[i].astype(F32) + got.astype(F32)).astype(BF16)
            return 0

        lax.fori_loop(0, groups // 2, one, 0)
        reduce_copy(0).start()
        reduce_copy(1).start()

    def add_relay():
        reduce_copy(0).wait_recv()
        got = fetch(second, 0, 0)
        part[2] = (part[2].astype(F32) + got.astype(F32)).astype(BF16)
        reduce_copy(2).start()

    def column(k):
        zc = plane(k)

        @pl.when(inside == 0)
        def _():
            column_arrived(zc)

        start(pass_on(k, 0, zc, j, near(k)))
        start(pass_on(k, 1, zc, j, next_one(k)))
        start(pass_on(k, 3, zc, j, mate))

    def relay(k):
        zc = plane(k)
        arrived(zc, near(k))
        start(pass_on(k, 2, zc, near(k), next_one(k)))
        start(pass_on(k, 4, zc, near(k), mate))
        arrived(zc, next_one(k))
        start(pass_on(k, 5, zc, next_one(k), mate))

    def slice_relay():
        arrived_slice(near(3))
        start(pass_slice(2, near(3), next_one(3)))
        start(pass_slice(4, near(3), mate))
        arrived_slice(next_one(3))
        start(pass_slice(5, next_one(3), mate))

    @pl.when(inside == 1)
    def _():
        forward(3, inner, outer)
        forward(2, outer, inner)
        for h in range(2):
            along_z(1, inner, outer, h).wait_recv()
            along_z(3, inner, outer, h).start()
            along_z(0, outer, outer, h).wait_recv()
            along_z(2, outer, inner, h).start()

    @pl.when(inside == 0)
    def _():
        slice_z(outer).wait_recv()
        info_z(0, outer, outer).wait_recv()

    relay(0)
    start(pass_slice(0, j, near(3)))
    start(pass_slice(1, j, next_one(3)))
    start(pass_slice(3, j, mate))

    def finish(i, s):
        gg[s] = acc_in[s, :, :feat].astype(BF16)
        gu[s] = acc_in[s, :, feat:].astype(BF16)
        gd[s] = acc_down[s].astype(BF16)

        @pl.when(i == 0)
        def _():
            for copy in swaps():
                copy.start()

    def slice_chunk():
        arrived_slice(mate)
        bring_slice(0).start()

        def pair(i, _):
            @pl.when(i < groups // 2 - 1)
            def _():
                arrived_slice(2 * chip_at(3, i + 1) + 1 - core)
                bring_slice(i + 1).start()

            bring_slice(i).wait()
            gather(outer, i, chip_at(3, i), cut // STRIPE)
            return 0

        lax.fori_loop(0, groups // 2, pair, 0)

        def take(i, _):
            s = experts - 1 - i
            for copy in send_acts(s):
                copy.wait_recv()
            for copy in take_acts(s):
                copy.start()
            return 0

        lax.fori_loop(0, experts, take, 0)

        def each(i, _):
            s = experts - 1 - i
            for copy in take_acts(s):
                copy.wait()
            mine = pl.ds(pl.multiple_of(s * 2 * cap, 16), 2 * cap)
            count = groups * cap
            x = xs[:, mine, pl.ds(0, cut)].reshape(count, cut)
            c = cs[:, mine, pl.ds(0, cut)].reshape(count, cut)
            acc_in[s] += dot(x, xs[s, :, pl.ds(cut, 2 * feat)], ((0,), (0,)))
            acc_down[s] += dot(c, xs[s, :, pl.ds(cut + 2 * feat, feat)], ((0,), (0,)))
            for copy in send_acts(s):
                copy.wait_send()
            if LATE:
                finish(i, s)
            return 0

        lax.fori_loop(0, experts, each, 0)

    def chunk(k, _):
        zc = plane(k)
        arrived(zc, mate)
        bring(k, 0).start()

        def pair(i, _):
            @pl.when(i == 2)
            def _():
                arrived(zc, far)
                start(pass_on(k, 6, zc, far, mate))

                @pl.when(k == 0)
                def _():
                    column(1)
                    slice_relay()

                    @pl.when(inside == 1)
                    def _():
                        forward(4, plane(2), outer)
                        for h in range(2):
                            along_z(1, plane(2), outer, h).wait_recv()
                            along_z(4, plane(2), outer, h).start()

                @pl.when(k == 1)
                def _():
                    relay(2)
                    arrived_slice(far)
                    start(pass_slice(6, far, mate))

            @pl.when(i < groups // 2 - 1)
            def _():
                arrived(zc, 2 * chip_at(k, i + 1) + 1 - core)
                bring(k, i + 1).start()

            bring(k, i).wait()
            gather(zc, i, chip_at(k, i), width // STRIPE)
            return 0

        lax.fori_loop(0, groups // 2, pair, 0)

        @pl.when(k == 0)
        def _():
            for copy in locals_[:3]:
                copy.wait()

        @pl.when(k == 2)
        def _():
            add_relay()

        def each(i, _):
            s = experts - 1 - i
            expert(k, s)

            @pl.when((k == 0) & (i == 1))
            def _():
                relay(1)
                column(2)

            if not LATE:
                @pl.when(k == 2)
                def _():
                    finish(i, s)

            return 0

        lax.fori_loop(0, experts, each, 0)

        @pl.when(k == 0)
        def _():
            lax.fori_loop(0, groups // 2, combine, 0)
            to_mate(2).wait_send()
            to_mate(3).wait_send()

        @pl.when(k == 1)
        def _():
            add_mate()
            if not LATE:
                slice_chunk()

        return 0

    lax.fori_loop(0, 3, chunk, 0)
    if LATE:
        slice_chunk()

    for which in (1, 2):
        reduce_copy(which).wait_recv()
    one, two = fetch(second, 1, 0).astype(F32), fetch(second, 2, 1).astype(F32)
    total = (part[0].astype(F32) + one + two).astype(BF16)
    mixed[...] = total[0]
    igrad[...] = total[1]
    for which in range(3):
        reduce_copy(which).wait_send()
    for copy in swaps():
        copy.wait_send()
    flag = flags[j % (groups // 2)]
    for m, (copy, ref) in enumerate(zip(swaps(), (gg, gu, gd))):
        copy.wait_recv()
        moved = jnp.full((cut, feat), flag) == 1
        ref[experts - 1] = jnp.where(
            moved, peer[m].astype(F32), ref[experts - 1].astype(F32)
        ).astype(BF16)
    for kind in range(7):
        for k in range(3):
            for copy in pass_on(k, kind, z, j, mate):
                copy.wait_send()
        for copy in pass_slice(kind, j, mate):
            copy.wait_send()
    info_z(0, z, outer).wait_send()

    @pl.when(inside == 0)
    def _():
        for h in range(2):
            along_z(0, z, outer, h).wait_send()

    @pl.when(inside == 1)
    def _():
        slice_z(z).wait_send()
        for slot in range(1, 5):
            info_z(slot, z, outer).wait_send()
            for h in range(2):
                along_z(slot, z, outer, h).wait_send()


def local_plane(tokens, cotangent, expert_ids, combine_weights, w_gate, w_up, w_down, swap_flags):
    toks, width = tokens.shape
    top = expert_ids.shape[1]
    experts, _, feat = w_gate.shape
    groups = lax.axis_size("expert")
    parts = lax.axis_size("dp")
    cap = toks * top * 5 // (4 * groups * experts)
    cut = width // parts
    rows = experts * 2 * cap
    chips = groups // 2
    own = jnp.stack([tokens, cotangent])
    info = jnp.concatenate([expert_ids.astype(F32), combine_weights], axis=1).T
    hbm = pl.BlockSpec(memory_space=pltpu.HBM)
    vmem = pl.BlockSpec(memory_space=pltpu.VMEM)
    smem = pl.BlockSpec(memory_space=pltpu.SMEM)
    sem = pltpu.SemaphoreType.DMA
    grad = jax.ShapeDtypeStruct((experts, cut, feat), BF16)
    out = jax.ShapeDtypeStruct((toks, width), BF16)
    results = pl.pallas_call(
        functools.partial(plane_kernel, cap),
        in_specs=[hbm, vmem, hbm, hbm, hbm, smem],
        out_specs=[vmem] * 5 + [hbm] * 4,
        out_shape=[
            out, out, grad, grad, grad,
            jax.ShapeDtypeStruct((parts, groups, 2, toks, width), BF16),
            jax.ShapeDtypeStruct((chips, 2, toks, width), BF16),
            jax.ShapeDtypeStruct((3, 2, toks, width), BF16),
            jax.ShapeDtypeStruct((3, experts, groups * cap, feat), BF16),
        ],
        scratch_shapes=[
            pltpu.VMEM((parts, groups, 2 * top, toks), F32),
            pltpu.VMEM((experts, width, 2 * feat), BF16),
            pltpu.VMEM((experts, width, feat), BF16),
            pltpu.VMEM((experts, cut, 2 * feat), F32),
            pltpu.VMEM((experts, cut, feat), F32),
            pltpu.VMEM((chips, rows, width), BF16),
            pltpu.VMEM((chips, rows, width), BF16),
            pltpu.VMEM((2, 2, 2, toks, width), BF16),
            pltpu.VMEM((chips, 2, toks, width), BF16),
            pltpu.VMEM((chips, rows, 2 * toks), BF16),
            pltpu.VMEM((chips, rows, 1), F32),
            pltpu.VMEM((3, cut, feat), BF16),
            sem((parts, 7)), sem((parts, 7)), sem((5, 2)), sem((5,)), sem((parts, 2)),
            sem((parts, groups)), sem((parts, groups)),
            sem((3, experts)), sem((3, experts)), sem((3, experts)),
            sem((5,)), sem((2,)), sem((chips,)), sem((chips,)),
            sem((3,)), sem((3,)), sem((3,)), sem((3,)),
        ],
        compiler_params=pltpu.CompilerParams(
            collective_id=0, has_side_effects=True, vmem_limit_bytes=KERNEL_VMEM
        ),
        cost_estimate=pl.CostEstimate(
            flops=60_000_000_000, bytes_accessed=100_000_000, transcendentals=5120 * feat
        ),
    )(own, info, w_gate, w_up, w_down, swap_flags)
    return tuple(results[:5])


def solution(mesh):
    small = mesh.shape["expert"] == 8 and mesh.shape["dp"] == 4
    return jax.shard_map(
        local_plane if small else local,
        mesh=mesh,
        in_specs=(
            P(("expert", "dp"), None),
            P(("expert", "dp"), None),
            P(("expert", "dp"), None),
            P(("expert", "dp"), None),
            P("expert", None, None),
            P("expert", None, None),
            P("expert", None, None),
            P(),
        ),
        out_specs=(
            P(("expert", "dp"), None),
            P(("expert", "dp"), None),
            P("expert", "dp", None),
            P("expert", "dp", None),
            P("expert", "dp", None),
        ),
        check_vma=False,
    )
```

```python
import functools

import jax
import jax.numpy as jnp
from jax import lax
from jax.experimental import pallas as pl
from jax.experimental.pallas import tpu as pltpu
from jax.sharding import PartitionSpec as P

F32 = jnp.float32
BF16 = jnp.bfloat16
VMEM_BYTES = 56 * 1024 * 1024


def dot(a, b, dims):
    return lax.dot_general(a, b, (dims, ((), ())), preferred_element_type=F32)


def forward_kernel(slot_ref, x_ref, wg_ref, wu_ref, wd_ref, out_ref, hid_ref, dgate_ref, dup_ref):
    x = x_ref[...]
    gate = dot(x, wg_ref[...], ((1,), (0,)))
    up = dot(x, wu_ref[...], ((1,), (0,)))
    s = jax.nn.sigmoid(gate)
    silu = gate * s
    hidden = (silu * up).astype(BF16)
    hid_ref[...] = hidden
    dgate_ref[...] = up * s * (1.0 + gate * (1.0 - s))
    dup_ref[...] = silu
    out_ref[...] = dot(hidden, wd_ref[...], ((1,), (1,))).astype(BF16)


def backward_kernel(
    slot_ref, c_ref, dgate_ref, dup_ref, wg_ref, wu_ref, wd_ref, term_ref, gc_ref, uc_ref
):
    hidden_cot = dot(c_ref[...], wd_ref[...], ((1,), (0,)))
    gate_cot = (hidden_cot * dgate_ref[...]).astype(BF16)
    up_cot = (hidden_cot * dup_ref[...]).astype(BF16)
    gc_ref[...] = gate_cot
    uc_ref[...] = up_cot
    term_ref[...] = (
        dot(gate_cot, wg_ref[...], ((1,), (1,))) + dot(up_cot, wu_ref[...], ((1,), (1,)))
    ).astype(BF16)


def grads_kernel(lhs_ref, *refs):
    lhs = lhs_ref[...]
    out_ref = refs[-1]
    for k, right_ref in enumerate(refs[:-1]):
        out_ref[0, k] = dot(lhs, right_ref[...], ((0,), (0,))).astype(BF16)


def expert_forward(slot, x, w_gate, w_up, w_down):
    rows, width = x.shape
    feat = w_gate.shape[2]
    tile = rows // 4
    weight = pl.BlockSpec((None, width, feat), lambda i, s: (s[0], 0, 0))
    wide = pl.BlockSpec((tile, width), lambda i, s: (i, 0))
    thin = pl.BlockSpec((tile, feat), lambda i, s: (i, 0))
    return pl.pallas_call(
        forward_kernel,
        grid_spec=pltpu.PrefetchScalarGridSpec(
            num_scalar_prefetch=1,
            grid=(rows // tile,),
            in_specs=[wide, weight, weight, weight],
            out_specs=[wide, thin, thin, thin],
        ),
        out_shape=[
            jax.ShapeDtypeStruct((rows, width), BF16),
            jax.ShapeDtypeStruct((rows, feat), BF16),
            jax.ShapeDtypeStruct((rows, feat), F32),
            jax.ShapeDtypeStruct((rows, feat), F32),
        ],
        compiler_params=pltpu.CompilerParams(vmem_limit_bytes=VMEM_BYTES),
        cost_estimate=pl.CostEstimate(
            flops=6 * rows * width * feat,
            bytes_accessed=4 * rows * width + 6 * width * feat + 10 * rows * feat,
            transcendentals=rows * feat,
        ),
    )(slot, x, w_gate, w_up, w_down)


def expert_backward(slot, c, dgate, dup, w_gate, w_up, w_down):
    rows, width = c.shape
    feat = w_gate.shape[2]
    tile = rows // 4
    weight = pl.BlockSpec((None, width, feat), lambda i, s: (s[0], 0, 0))
    wide = pl.BlockSpec((tile, width), lambda i, s: (i, 0))
    thin = pl.BlockSpec((tile, feat), lambda i, s: (i, 0))
    return pl.pallas_call(
        backward_kernel,
        grid_spec=pltpu.PrefetchScalarGridSpec(
            num_scalar_prefetch=1,
            grid=(rows // tile,),
            in_specs=[wide, thin, thin, weight, weight, weight],
            out_specs=[wide, thin, thin],
        ),
        out_shape=[
            jax.ShapeDtypeStruct((rows, width), BF16),
            jax.ShapeDtypeStruct((rows, feat), BF16),
            jax.ShapeDtypeStruct((rows, feat), BF16),
        ],
        compiler_params=pltpu.CompilerParams(vmem_limit_bytes=VMEM_BYTES),
        cost_estimate=pl.CostEstimate(
            flops=6 * rows * width * feat,
            bytes_accessed=4 * rows * width + 6 * width * feat + 12 * rows * feat,
            transcendentals=0,
        ),
    )(slot, c, dgate, dup, w_gate, w_up, w_down)


def expert_grads(lhs, rights, parts):
    rows, width = lhs.shape
    feat = rights[0].shape[1]
    number = len(rights)
    cols = width // parts
    thin = pl.BlockSpec((rows, feat), lambda i: (0, 0))
    return pl.pallas_call(
        grads_kernel,
        grid=(parts,),
        in_specs=[pl.BlockSpec((rows, cols), lambda i: (0, i))] + [thin] * number,
        out_specs=pl.BlockSpec((1, number, cols, feat), lambda i: (i, 0, 0, 0)),
        out_shape=jax.ShapeDtypeStruct((parts, number, cols, feat), BF16),
        compiler_params=pltpu.CompilerParams(vmem_limit_bytes=VMEM_BYTES),
        cost_estimate=pl.CostEstimate(
            flops=2 * number * rows * width * feat,
            bytes_accessed=2 * rows * width + 2 * number * (width + rows) * feat,
            transcendentals=0,
        ),
    )(lhs, *rights)


def local(tokens, cotangent, expert_ids, combine_weights, w_gate, w_up, w_down, swap_flags):
    tok_rows, width = tokens.shape
    top_count = expert_ids.shape[1]
    per_device = w_gate.shape[0]
    groups = lax.axis_size("expert")
    parts = lax.axis_size("dp")
    half = groups // 2
    experts_all = groups * per_device
    capacity = tok_rows * top_count * 5 // (4 * experts_all) * parts
    total = groups * capacity
    mine = lax.axis_index("dp")
    slot = mine.astype(jnp.int32).reshape(1)

    info = jnp.concatenate([expert_ids.astype(F32), combine_weights], axis=1)
    info = lax.all_gather(info, "dp", tiled=True)
    tok_all = lax.all_gather(tokens, "dp", tiled=True)
    cot_all = lax.all_gather(cotangent, "dp", tiled=True)
    ids = info[:, :top_count].astype(jnp.int32)
    weights = info[:, top_count:]
    count = ids.shape[0]
    wanted = jnp.arange(groups, dtype=jnp.int32) * per_device + mine
    match = ids[:, :, None] == wanted[None, None, :]
    hit = jnp.any(match, axis=1)
    route_weight = jnp.sum(jnp.where(match, weights[:, :, None], 0.0), axis=1)
    below = (jnp.arange(count)[:, None] > jnp.arange(count)[None, :]).astype(BF16)
    rank = dot(below, hit.astype(BF16), ((1,), (0,))).astype(jnp.int32)
    place = jnp.where(hit, rank, -1).T
    picked = place[:, None, :] == jnp.arange(capacity, dtype=jnp.int32)[None, :, None]
    row_weight = jnp.sum(jnp.where(picked, route_weight.T[:, None, :], 0.0), axis=2).reshape(total, 1)
    pick = picked.astype(BF16).reshape(total, count)
    pick_weighted = (
        jnp.where(picked, route_weight.T[:, None, :], 0.0).astype(BF16).reshape(total, count)
    )

    def exchange(value):
        shape = (groups, capacity, width)
        return lax.all_to_all(
            value.reshape(shape), "expert", split_axis=0, concat_axis=0, tiled=True
        ).reshape(total, width)

    x = exchange(dot(pick, tok_all, ((1,), (0,))).astype(BF16))
    c = exchange((dot(pick, cot_all, ((1,), (0,))) * row_weight).astype(BF16))
    out, hidden, dgate, dup = expert_forward(slot, x, w_gate, w_up, w_down)
    out_back = exchange(out)

    def blocks(grads):
        return [
            lax.dynamic_index_in_dim(grads, mine ^ step, keepdims=False) for step in range(parts)
        ]

    def swap(block, step):
        return lax.ppermute(block, "dp", [(i, i ^ step) for i in range(parts)])

    down = blocks(expert_grads(c, [hidden], parts))
    dgate, *down = lax.optimization_barrier((dgate, *down))
    down = down[:1] + [swap(down[step], step) for step in range(1, parts)]
    term, gate_cot, up_cot = expert_backward(slot, c, dgate, dup, w_gate, w_up, w_down)
    both = blocks(expert_grads(x, [gate_cot, up_cot], parts))
    both[0], *moved = lax.optimization_barrier((both[0], *both[1:], *down[1:]))
    both, down = both[:1] + moved[: parts - 1], down[:1] + moved[parts - 1 :]
    both = both[:1] + [swap(both[step], step) for step in range(1, parts)]
    term, *ready = lax.optimization_barrier((term, *down, *both[:-1]))
    term_back = exchange(term)
    term_back, final = lax.optimization_barrier((term_back, both[-1]))
    down, both = ready[:parts], [*ready[parts:], final]
    received = [jnp.concatenate([b, d], axis=0) for b, d in zip(both, down)]

    mixed_part = dot(pick_weighted, out_back, ((0,), (0,))).astype(BF16)
    mixed = lax.psum_scatter(mixed_part, "dp", scatter_dimension=0, tiled=True)
    input_part = dot(pick, term_back, ((0,), (0,))).astype(BF16)
    input_grad = lax.psum_scatter(input_part, "dp", scatter_dimension=0, tiled=True)

    last = lax.select_n((per_device - 1) ^ mine, *received)
    pairs = [(i, (i + half) % groups) for i in range(groups)]
    peer = lax.ppermute(last, "expert", pairs)
    pair = lax.axis_index("expert") % half
    flag = jnp.sum(jnp.where(jnp.arange(half) == pair, swap_flags, 0)) == 1
    chosen = jnp.where(flag, peer, last)
    out_grads = []
    for m in range(3):
        whole = jnp.zeros((per_device,) + last.shape[1:], BF16)
        for step in range(parts):
            whole = lax.dynamic_update_index_in_dim(whole, received[step][m], mine ^ step, 0)
        out_grads.append(whole.at[per_device - 1].set(chosen[m]))
    return (mixed, input_grad, *out_grads)


MESH = pl.DeviceIdType.MESH
KERNEL_VMEM = 62 * 1024 * 1024
STRIPE = 512
LATE = True


def plane_kernel(
    cap,
    tokens, cotangent, names, weighing, wg, wu, wd,
    mixed, igrad, gg, gu, gd, everyone, first, second, acts, peer,
    infos, wgu, wdv, acc_in, acc_down, xs, cs, stage, part, picks, row_weights,
    send_block, send_info, send_z, send_zinfo, recv_column, recv_block, recv_info, send_act, recv_act, act_sem,
    local_sem, stage_sem, send_first, recv_first, send_second, recv_second, send_swap, recv_swap,
):
    parts, groups = everyone.shape[0], everyone.shape[1]
    toks, width = tokens.shape
    own = part.at[0]
    experts, _, feat = wg.shape
    top = names.shape[0]
    cut = width // parts
    rows = experts * 2 * cap
    j = lax.axis_index("expert")
    z = lax.axis_index("dp")
    core = j % 2
    chip = j // 2
    across_x = (j // 4) * 4 + (1 - chip % 2) * 2 + core
    across_y = (1 - j // 4) * 4 + (chip % 2) * 2 + core
    mate = j + 1 - 2 * core
    def near(k):
        swung = jnp.where(k == 2, 1, core)
        return across_x + swung * (across_y - across_x)

    def next_one(k):
        swung = jnp.where(k == 2, 1, core)
        return across_y + swung * (across_x - across_y)

    far = (3 - chip) * 2 + core
    half = z // 2
    outer = z + 1 - 2 * (z % 2)
    inner = 3 - z
    inside = (z + half) % 2

    here = pl.ds(pl.multiple_of(z * cut, cut), cut)

    def plane(k):
        return jnp.where(
            k == 0, z, jnp.where(k == 1, 2 - half, jnp.where(k == 2, 3 - 3 * half, outer))
        )

    barrier = pltpu.get_barrier_semaphore()
    for other in (across_x, across_y, mate):
        pl.semaphore_signal(barrier, inc=1, device_id=(other, z), device_id_type=MESH)
    pl.semaphore_signal(barrier, inc=1, device_id=(j, outer), device_id_type=MESH)

    @pl.when(inside == 1)
    def _():
        pl.semaphore_signal(barrier, inc=1, device_id=(j, inner), device_id_type=MESH)

    locals_ = [
        pltpu.make_async_copy(wg, wgu.at[:, :, pl.ds(0, feat)], local_sem.at[0]),
        pltpu.make_async_copy(wu, wgu.at[:, :, pl.ds(feat, feat)], local_sem.at[1]),
        pltpu.make_async_copy(wd, wdv, local_sem.at[2]),
        pltpu.make_async_copy(tokens, part.at[0, 0], local_sem.at[3]),
        pltpu.make_async_copy(cotangent, part.at[0, 1], local_sem.at[4]),
        pltpu.make_async_copy(own, everyone.at[z, j], local_sem.at[5]),
    ]
    locals_[3].start()
    locals_[4].start()
    infos[z, j, pl.ds(0, top)] = names[...].astype(F32)
    infos[z, j, pl.ds(top, top)] = weighing[...]
    locals_[3].wait()
    locals_[4].wait()
    pl.semaphore_wait(barrier, 4 + inside)

    def remote(src, dst, send, recv, to, row=None):
        return pltpu.make_async_remote_copy(
            src_ref=src, dst_ref=dst, send_sem=send, recv_sem=recv,
            device_id=(to, z if row is None else row), device_id_type=MESH,
        )

    def pass_on(k, kind, zc, block, to, source=None, source_info=None):
        return (
            remote(
                everyone.at[zc, block] if source is None else source,
                everyone.at[zc, block],
                send_block.at[k, kind], recv_block.at[zc, block], to,
            ),
            remote(
                infos.at[zc, block] if source_info is None else source_info,
                infos.at[zc, block],
                send_info.at[k, kind], recv_info.at[zc, block], to,
            ),
        )

    def pass_slice(kind, block, to):
        ref = everyone.at[outer, block, :, :, here]
        return (
            remote(ref, ref, send_block.at[3, kind], recv_block.at[outer, block], to),
            remote(
                infos.at[outer, block], infos.at[outer, block],
                send_info.at[3, kind], recv_info.at[outer, block], to,
            ),
        )

    def send_acts(s):
        return [
            remote(
                ref.at[s, pl.ds(0, groups * cap)], acts.at[m, s],
                send_act.at[m, s], recv_act.at[m, s], j, outer,
            )
            for m, ref in enumerate((gg, gu, gd))
        ]

    def take_acts(s):
        return [
            pltpu.make_async_copy(
                acts.at[m, s], xs.at[s, :, pl.ds(cut + m * feat, feat)], act_sem.at[m, s]
            )
            for m in range(3)
        ]

    def along_z(slot, zc, to, h, source=None):
        return remote(
            everyone.at[zc, j, h] if source is None else source.at[h],
            everyone.at[zc, j, h],
            send_z.at[slot, h], recv_column.at[zc, h], j, to,
        )

    def info_z(slot, zc, to, source=None):
        return remote(
            infos.at[zc, j] if source is None else source,
            infos.at[zc, j],
            send_zinfo.at[slot], recv_info.at[zc, j], j, to,
        )

    def slice_z(zc, source=None):
        there = pl.ds(pl.multiple_of((z + outer - zc) * cut, cut), cut)
        return remote(
            everyone.at[zc, j, :, :, there] if source is None else source.at[:, :, there],
            everyone.at[zc, j, :, :, there],
            send_z.at[0, 0], recv_column.at[zc, 0], j, outer,
        )

    def column_arrived(zc):
        for h in range(2):
            along_z(0, zc, outer, h).wait_recv()
        info_z(0, zc, outer).wait_recv()

    def forward(slot, zc, to):
        info_z(0, zc, outer).wait_recv()
        info_z(slot, zc, to).start()

    def start(pair):
        pair[0].start()
        pair[1].start()

    def arrived(zc, block):
        for copy in pass_on(0, 0, zc, block, mate):
            copy.wait_recv()

    def arrived_slice(block):
        for copy in pass_slice(0, block, mate):
            copy.wait_recv()

    start(pass_on(0, 0, z, j, near(0), own))
    start(pass_on(0, 1, z, j, next_one(0), own))
    info_z(0, z, outer).start()

    @pl.when(inside == 0)
    def _():
        for h in range(2):
            along_z(0, z, outer, h, own).start()

    @pl.when(inside == 1)
    def _():
        slice_z(z, own).start()
        info_z(1, z, inner).start()
        for h in range(2):
            along_z(1, z, inner, h, own).start()

    start(pass_on(0, 3, z, j, mate, own))
    locals_[5].start()
    for copy in locals_[:3]:
        copy.start()
    acc_in[...] = jnp.zeros_like(acc_in)
    acc_down[...] = jnp.zeros_like(acc_down)
    locals_[5].wait()

    def chip_at(k, i):
        return jnp.where(
            i == 0,
            chip,
            jnp.where(i == 1, near(k) // 2, jnp.where(i == 2, next_one(k) // 2, far // 2)),
        )

    def bring(k, i):
        return pltpu.make_async_copy(
            everyone.at[plane(k), pl.ds(2 * chip_at(k, i), 2)], stage.at[i % 2], stage_sem.at[i % 2]
        )

    def bring_slice(i):
        return pltpu.make_async_copy(
            everyone.at[outer, pl.ds(2 * chip_at(3, i), 2), :, :, here],
            stage.at[i % 2, :, :, :, pl.ds(0, cut)],
            stage_sem.at[i % 2],
        )

    def gather(zc, i, at, stripes):
        hits, weights = [], []
        for s in range(experts):
            name = (experts * j + s).astype(F32)
            for b in range(2):
                table = infos[zc, 2 * at + b]
                match = table[:top] == name
                hits.append(jnp.sum(jnp.where(match, 1.0, 0.0), axis=0, keepdims=True))
                weights.append(jnp.sum(jnp.where(match, table[top:], 0.0), axis=0, keepdims=True))
        hit = jnp.concatenate(hits, axis=0)
        before = (
            lax.broadcasted_iota(jnp.int32, (toks, toks), 0)
            < lax.broadcasted_iota(jnp.int32, (toks, toks), 1)
        )
        rank = dot(hit.astype(BF16), jnp.where(before, 1.0, 0.0).astype(BF16), ((1,), (0,)))
        line = lax.broadcasted_iota(jnp.int32, (2 * cap, 2 * toks), 0).astype(F32)
        chosen, scales = [], []
        for s in range(experts):
            place = jnp.concatenate(
                [
                    jnp.where(hits[2 * s + b] > 0, rank[2 * s + b : 2 * s + b + 1] + cap * b, -1.0)
                    for b in range(2)
                ],
                axis=1,
            )
            weight = jnp.concatenate(weights[2 * s : 2 * s + 2], axis=1)
            same = line == place
            chosen.append(jnp.where(same, 1.0, 0.0).astype(BF16))
            scales.append(jnp.sum(jnp.where(same, weight, 0.0), axis=1, keepdims=True))
        pick = jnp.concatenate(chosen, axis=0)
        scale = jnp.concatenate(scales, axis=0)
        picks[i] = pick
        row_weights[i] = scale
        for n in range(stripes):
            cols = pl.ds(n * STRIPE, STRIPE)
            tok = stage[i % 2, :, 0, :, cols].reshape(2 * toks, STRIPE)
            xs[i, :, cols] = dot(pick, tok, ((1,), (0,))).astype(BF16)
            cot = stage[i % 2, :, 1, :, cols].reshape(2 * toks, STRIPE)
            cs[i, :, cols] = (dot(pick, cot, ((1,), (0,))) * scale).astype(BF16)

    def expert(k, s):
        mine = pl.ds(pl.multiple_of(s * 2 * cap, 16), 2 * cap)
        count = groups * cap
        x = xs[:, mine, :].reshape(count, width)
        both = dot(x, wgu[s], ((1,), (0,)))
        c = cs[:, mine, :].reshape(count, width)
        hidden_cot = dot(c, wdv[s], ((1,), (0,)))
        gate, up = both[:, :feat], both[:, feat:]
        sig = jax.nn.sigmoid(gate)
        silu = gate * sig
        hidden = (silu * up).astype(BF16)
        cots = jnp.concatenate(
            [
                (hidden_cot * up * sig * (1.0 + gate * (1.0 - sig))).astype(BF16),
                (hidden_cot * silu).astype(BF16),
            ],
            axis=1,
        )
        acc_in[s] += dot(xs[:, mine, here].reshape(count, cut), cots, ((0,), (0,)))
        acc_down[s] += dot(cs[:, mine, here].reshape(count, cut), hidden, ((0,), (0,)))

        @pl.when(k == 0)
        def _():
            gg[s, pl.ds(0, count)] = cots[:, :feat]
            gu[s, pl.ds(0, count)] = cots[:, feat:]
            gd[s, pl.ds(0, count)] = hidden
            for copy in send_acts(s):
                copy.start()
            scale = row_weights[:, mine, :].reshape(count, 1)
            for n in range(width // STRIPE):
                cols = pl.ds(n * STRIPE, STRIPE)
                out = dot(hidden, wdv[s, cols, :], ((1,), (1,))) * scale
                xs[:, mine, cols] = out.astype(BF16).reshape(groups // 2, 2 * cap, STRIPE)
                term = dot(cots, wgu[s, cols, :], ((1,), (1,)))
                cs[:, mine, cols] = term.astype(BF16).reshape(groups // 2, 2 * cap, STRIPE)

    def swaps():
        last = experts - 1
        return [
            remote(ref.at[last], peer.at[m], send_swap.at[m], recv_swap.at[m], across_y)
            for m, ref in enumerate((gg, gu, gd))
        ]

    def to_mate(i):
        there = (2 * i) % 3 + 3 * (i // 3)
        return remote(
            stage.at[i % 2, 1 - core], first.at[there], send_first.at[i], recv_first.at[there], mate
        )

    def from_mate(i):
        return remote(
            stage.at[i % 2, 1 - core], first.at[i], send_first.at[i], recv_first.at[i], mate
        )

    def combine(i, _):
        @pl.when(i >= 2)
        def _():
            to_mate(i - 2).wait_send()

        for n in range(width // STRIPE):
            cols = pl.ds(n * STRIPE, STRIPE)
            for a, ref in enumerate((xs, cs)):
                total = dot(picks[i], ref[i, :, cols], ((0,), (0,))).astype(BF16)
                stage[i % 2, :, a, :, cols] = total.reshape(2, toks, STRIPE)
        to_mate(i).start()
        part[i] = stage[i % 2, core]
        return 0

    def reduce_copy(which):
        source, to = ((3, near(0)), (1, near(0)), (2, next_one(0)))[which]
        return remote(
            part.at[source], second.at[which], send_second.at[which],
            recv_second.at[which], to,
        )

    def fetch(ref, at, slot):
        copy = pltpu.make_async_copy(ref.at[at], stage.at[slot, 0], stage_sem.at[slot])
        copy.start()
        copy.wait()
        return stage[slot, 0]

    def add_mate():
        def one(i, _):
            from_mate(i).wait_recv()
            got = fetch(first, i, 0)
            part[i] = (part[i].astype(F32) + got.astype(F32)).astype(BF16)
            return 0

        lax.fori_loop(0, groups // 2, one, 0)
        reduce_copy(0).start()
        reduce_copy(1).start()

    def add_relay():
        reduce_copy(0).wait_recv()
        got = fetch(second, 0, 0)
        part[2] = (part[2].astype(F32) + got.astype(F32)).astype(BF16)
        reduce_copy(2).start()

    def column(k):
        zc = plane(k)

        @pl.when(inside == 0)
        def _():
            column_arrived(zc)

        start(pass_on(k, 0, zc, j, near(k)))
        start(pass_on(k, 1, zc, j, next_one(k)))
        start(pass_on(k, 3, zc, j, mate))

    def relay(k):
        zc = plane(k)
        arrived(zc, near(k))
        start(pass_on(k, 2, zc, near(k), next_one(k)))
        start(pass_on(k, 4, zc, near(k), mate))
        arrived(zc, next_one(k))
        start(pass_on(k, 5, zc, next_one(k), mate))

    def slice_relay():
        arrived_slice(near(3))
        start(pass_slice(2, near(3), next_one(3)))
        start(pass_slice(4, near(3), mate))
        arrived_slice(next_one(3))
        start(pass_slice(5, next_one(3), mate))

    @pl.when(inside == 1)
    def _():
        forward(3, inner, outer)
        forward(2, outer, inner)
        for h in range(2):
            along_z(1, inner, outer, h).wait_recv()
            along_z(3, inner, outer, h).start()
            along_z(0, outer, outer, h).wait_recv()
            along_z(2, outer, inner, h).start()

    @pl.when(inside == 0)
    def _():
        slice_z(outer).wait_recv()
        info_z(0, outer, outer).wait_recv()

    relay(0)
    start(pass_slice(0, j, near(3)))
    start(pass_slice(1, j, next_one(3)))
    start(pass_slice(3, j, mate))

    def finish(i, s):
        gg[s] = acc_in[s, :, :feat].astype(BF16)
        gu[s] = acc_in[s, :, feat:].astype(BF16)
        gd[s] = acc_down[s].astype(BF16)

        @pl.when(i == 0)
        def _():
            for copy in swaps():
                copy.start()

    def slice_chunk():
        arrived_slice(mate)
        bring_slice(0).start()

        def pair(i, _):
            @pl.when(i < groups // 2 - 1)
            def _():
                arrived_slice(2 * chip_at(3, i + 1) + 1 - core)
                bring_slice(i + 1).start()

            bring_slice(i).wait()
            gather(outer, i, chip_at(3, i), cut // STRIPE)
            return 0

        lax.fori_loop(0, groups // 2, pair, 0)

        def take(i, _):
            s = experts - 1 - i
            for copy in send_acts(s):
                copy.wait_recv()
            for copy in take_acts(s):
                copy.start()
            return 0

        lax.fori_loop(0, experts, take, 0)

        def each(i, _):
            s = experts - 1 - i
            for copy in take_acts(s):
                copy.wait()
            mine = pl.ds(pl.multiple_of(s * 2 * cap, 16), 2 * cap)
            count = groups * cap
            x = xs[:, mine, pl.ds(0, cut)].reshape(count, cut)
            c = cs[:, mine, pl.ds(0, cut)].reshape(count, cut)
            acc_in[s] += dot(x, xs[s, :, pl.ds(cut, 2 * feat)], ((0,), (0,)))
            acc_down[s] += dot(c, xs[s, :, pl.ds(cut + 2 * feat, feat)], ((0,), (0,)))
            for copy in send_acts(s):
                copy.wait_send()
            if LATE:
                finish(i, s)
            return 0

        lax.fori_loop(0, experts, each, 0)

    def chunk(k, _):
        zc = plane(k)
        arrived(zc, mate)
        bring(k, 0).start()

        def pair(i, _):
            @pl.when(i == 2)
            def _():
                arrived(zc, far)
                start(pass_on(k, 6, zc, far, mate))

                @pl.when(k == 0)
                def _():
                    column(1)
                    slice_relay()

                    @pl.when(inside == 1)
                    def _():
                        forward(4, plane(2), outer)
                        for h in range(2):
                            along_z(1, plane(2), outer, h).wait_recv()
                            along_z(4, plane(2), outer, h).start()

                @pl.when(k == 1)
                def _():
                    relay(2)
                    arrived_slice(far)
                    start(pass_slice(6, far, mate))

            @pl.when(i < groups // 2 - 1)
            def _():
                arrived(zc, 2 * chip_at(k, i + 1) + 1 - core)
                bring(k, i + 1).start()

            bring(k, i).wait()
            gather(zc, i, chip_at(k, i), width // STRIPE)
            return 0

        lax.fori_loop(0, groups // 2, pair, 0)

        @pl.when(k == 0)
        def _():
            for copy in locals_[:3]:
                copy.wait()

        @pl.when(k == 2)
        def _():
            add_relay()

        def each(i, _):
            s = experts - 1 - i
            expert(k, s)

            @pl.when((k == 0) & (i == 1))
            def _():
                relay(1)
                column(2)

            if not LATE:
                @pl.when(k == 2)
                def _():
                    finish(i, s)

            return 0

        lax.fori_loop(0, experts, each, 0)

        @pl.when(k == 0)
        def _():
            for kind in (0, 1, 3):
                for copy in pass_on(0, kind, z, j, mate, own):
                    copy.wait_send()

            @pl.when(inside == 0)
            def _():
                for h in range(2):
                    along_z(0, z, outer, h, own).wait_send()

            @pl.when(inside == 1)
            def _():
                slice_z(z, own).wait_send()
                for h in range(2):
                    along_z(1, z, inner, h, own).wait_send()

            lax.fori_loop(0, groups // 2, combine, 0)
            to_mate(2).wait_send()
            to_mate(3).wait_send()

        @pl.when(k == 1)
        def _():
            add_mate()
            if not LATE:
                slice_chunk()

        return 0

    lax.fori_loop(0, 3, chunk, 0)
    if LATE:
        slice_chunk()

    for which in (1, 2):
        reduce_copy(which).wait_recv()
    one, two = fetch(second, 1, 0).astype(F32), fetch(second, 2, 1).astype(F32)
    total = (part[0].astype(F32) + one + two).astype(BF16)
    mixed[...] = total[0]
    igrad[...] = total[1]
    for which in range(3):
        reduce_copy(which).wait_send()
    for copy in swaps():
        copy.wait_send()
    for copy in swaps():
        copy.wait_recv()
    for kind in range(7):
        for k in range(3):
            if k or kind not in (0, 1, 3):
                for copy in pass_on(k, kind, z, j, mate):
                    copy.wait_send()
        for copy in pass_slice(kind, j, mate):
            copy.wait_send()
    info_z(0, z, outer).wait_send()

    @pl.when(inside == 1)
    def _():
        for slot in range(1, 5):
            info_z(slot, z, outer).wait_send()
        for slot in range(2, 5):
            for h in range(2):
                along_z(slot, z, outer, h).wait_send()


def settle_kernel(flag, mixed, igrad, gg, gu, gd, peer, out_mixed, out_igrad, *outs):
    out_mixed[...] = mixed[...]
    out_igrad[...] = igrad[...]
    moved = (pl.program_id(0) == pl.num_programs(0) - 1) & (flag[0] == 1)
    for m, (ref, out) in enumerate(zip((gg, gu, gd), outs)):
        out[...] = ref[...]

        @pl.when(moved)
        def _():
            out[...] = peer[m]


def local_plane(tokens, cotangent, expert_ids, combine_weights, w_gate, w_up, w_down, swap_flags):
    toks, width = tokens.shape
    top = expert_ids.shape[1]
    experts, _, feat = w_gate.shape
    groups = lax.axis_size("expert")
    parts = lax.axis_size("dp")
    cap = toks * top * 5 // (4 * groups * experts)
    cut = width // parts
    rows = experts * 2 * cap
    chips = groups // 2
    hbm = pl.BlockSpec(memory_space=pltpu.HBM)
    vmem = pl.BlockSpec(memory_space=pltpu.VMEM)
    sem = pltpu.SemaphoreType.DMA
    grad = jax.ShapeDtypeStruct((experts, cut, feat), BF16)
    out = jax.ShapeDtypeStruct((toks, width), BF16)
    results = pl.pallas_call(
        functools.partial(plane_kernel, cap),
        in_specs=[hbm, hbm, vmem, vmem, hbm, hbm, hbm],
        out_specs=[vmem] * 5 + [hbm] * 5,
        out_shape=[
            out, out, grad, grad, grad,
            jax.ShapeDtypeStruct((parts, groups, 2, toks, width), BF16),
            jax.ShapeDtypeStruct((chips, 2, toks, width), BF16),
            jax.ShapeDtypeStruct((3, 2, toks, width), BF16),
            jax.ShapeDtypeStruct((3, experts, groups * cap, feat), BF16),
            jax.ShapeDtypeStruct((3, cut, feat), BF16),
        ],
        scratch_shapes=[
            pltpu.VMEM((parts, groups, 2 * top, toks), F32),
            pltpu.VMEM((experts, width, 2 * feat), BF16),
            pltpu.VMEM((experts, width, feat), BF16),
            pltpu.VMEM((experts, cut, 2 * feat), F32),
            pltpu.VMEM((experts, cut, feat), F32),
            pltpu.VMEM((chips, rows, width), BF16),
            pltpu.VMEM((chips, rows, width), BF16),
            pltpu.VMEM((2, 2, 2, toks, width), BF16),
            pltpu.VMEM((chips, 2, toks, width), BF16),
            pltpu.VMEM((chips, rows, 2 * toks), BF16),
            pltpu.VMEM((chips, rows, 1), F32),
            sem((parts, 7)), sem((parts, 7)), sem((5, 2)), sem((5,)), sem((parts, 2)),
            sem((parts, groups)), sem((parts, groups)),
            sem((3, experts)), sem((3, experts)), sem((3, experts)),
            sem((6,)), sem((2,)), sem((chips,)), sem((chips,)),
            sem((3,)), sem((3,)), sem((3,)), sem((3,)),
        ],
        compiler_params=pltpu.CompilerParams(
            collective_id=0, has_side_effects=True, vmem_limit_bytes=KERNEL_VMEM
        ),
        cost_estimate=pl.CostEstimate(
            flops=60_000_000_000, bytes_accessed=100_000_000, transcendentals=5120 * feat
        ),
    )(tokens, cotangent, expert_ids.T, combine_weights.T, w_gate, w_up, w_down)
    pair = lax.axis_index("expert") % (groups // 2)
    flag = jnp.sum(jnp.where(jnp.arange(groups // 2) == pair, swap_flags, 0))
    lines = pl.BlockSpec((toks // experts, width), lambda i, f: (i, 0))
    panel = pl.BlockSpec((None, cut, feat), lambda i, f: (i, 0, 0))
    whole = pl.BlockSpec((3, cut, feat), lambda i, f: (0, 0, 0))
    return pl.pallas_call(
        settle_kernel,
        grid_spec=pltpu.PrefetchScalarGridSpec(
            num_scalar_prefetch=1,
            grid=(experts,),
            in_specs=[lines, lines, panel, panel, panel, whole],
            out_specs=[lines, lines, panel, panel, panel],
        ),
        out_shape=[out, out, grad, grad, grad],
        compiler_params=pltpu.CompilerParams(vmem_limit_bytes=KERNEL_VMEM),
    )(flag.reshape(1), *results[:5], results[9])


def solution(mesh):
    small = mesh.shape["expert"] == 8 and mesh.shape["dp"] == 4
    return jax.shard_map(
        local_plane if small else local,
        mesh=mesh,
        in_specs=(
            P(("expert", "dp"), None),
            P(("expert", "dp"), None),
            P(("expert", "dp"), None),
            P(("expert", "dp"), None),
            P("expert", None, None),
            P("expert", None, None),
            P("expert", None, None),
            P(),
        ),
        out_specs=(
            P(("expert", "dp"), None),
            P(("expert", "dp"), None),
            P("expert", "dp", None),
            P("expert", "dp", None),
            P("expert", "dp", None),
        ),
        check_vma=False,
    )
```

```python
import functools

import jax
import jax.numpy as jnp
from jax import lax
from jax.experimental import pallas as pl
from jax.experimental.pallas import tpu as pltpu
from jax.sharding import PartitionSpec as P

F32 = jnp.float32
BF16 = jnp.bfloat16
VMEM_BYTES = 56 * 1024 * 1024


def dot(a, b, dims):
    return lax.dot_general(a, b, (dims, ((), ())), preferred_element_type=F32)


def forward_kernel(slot_ref, x_ref, wg_ref, wu_ref, wd_ref, out_ref, hid_ref, dgate_ref, dup_ref):
    x = x_ref[...]
    gate = dot(x, wg_ref[...], ((1,), (0,)))
    up = dot(x, wu_ref[...], ((1,), (0,)))
    s = jax.nn.sigmoid(gate)
    silu = gate * s
    hidden = (silu * up).astype(BF16)
    hid_ref[...] = hidden
    dgate_ref[...] = up * s * (1.0 + gate * (1.0 - s))
    dup_ref[...] = silu
    out_ref[...] = dot(hidden, wd_ref[...], ((1,), (1,))).astype(BF16)


def backward_kernel(
    slot_ref, c_ref, dgate_ref, dup_ref, wg_ref, wu_ref, wd_ref, term_ref, gc_ref, uc_ref
):
    hidden_cot = dot(c_ref[...], wd_ref[...], ((1,), (0,)))
    gate_cot = (hidden_cot * dgate_ref[...]).astype(BF16)
    up_cot = (hidden_cot * dup_ref[...]).astype(BF16)
    gc_ref[...] = gate_cot
    uc_ref[...] = up_cot
    term_ref[...] = (
        dot(gate_cot, wg_ref[...], ((1,), (1,))) + dot(up_cot, wu_ref[...], ((1,), (1,)))
    ).astype(BF16)


def grads_kernel(lhs_ref, *refs):
    lhs = lhs_ref[...]
    out_ref = refs[-1]
    for k, right_ref in enumerate(refs[:-1]):
        out_ref[0, k] = dot(lhs, right_ref[...], ((0,), (0,))).astype(BF16)


def expert_forward(slot, x, w_gate, w_up, w_down):
    rows, width = x.shape
    feat = w_gate.shape[2]
    tile = rows // 4
    weight = pl.BlockSpec((None, width, feat), lambda i, s: (s[0], 0, 0))
    wide = pl.BlockSpec((tile, width), lambda i, s: (i, 0))
    thin = pl.BlockSpec((tile, feat), lambda i, s: (i, 0))
    return pl.pallas_call(
        forward_kernel,
        grid_spec=pltpu.PrefetchScalarGridSpec(
            num_scalar_prefetch=1,
            grid=(rows // tile,),
            in_specs=[wide, weight, weight, weight],
            out_specs=[wide, thin, thin, thin],
        ),
        out_shape=[
            jax.ShapeDtypeStruct((rows, width), BF16),
            jax.ShapeDtypeStruct((rows, feat), BF16),
            jax.ShapeDtypeStruct((rows, feat), F32),
            jax.ShapeDtypeStruct((rows, feat), F32),
        ],
        compiler_params=pltpu.CompilerParams(vmem_limit_bytes=VMEM_BYTES),
        cost_estimate=pl.CostEstimate(
            flops=6 * rows * width * feat,
            bytes_accessed=4 * rows * width + 6 * width * feat + 10 * rows * feat,
            transcendentals=rows * feat,
        ),
    )(slot, x, w_gate, w_up, w_down)


def expert_backward(slot, c, dgate, dup, w_gate, w_up, w_down):
    rows, width = c.shape
    feat = w_gate.shape[2]
    tile = rows // 4
    weight = pl.BlockSpec((None, width, feat), lambda i, s: (s[0], 0, 0))
    wide = pl.BlockSpec((tile, width), lambda i, s: (i, 0))
    thin = pl.BlockSpec((tile, feat), lambda i, s: (i, 0))
    return pl.pallas_call(
        backward_kernel,
        grid_spec=pltpu.PrefetchScalarGridSpec(
            num_scalar_prefetch=1,
            grid=(rows // tile,),
            in_specs=[wide, thin, thin, weight, weight, weight],
            out_specs=[wide, thin, thin],
        ),
        out_shape=[
            jax.ShapeDtypeStruct((rows, width), BF16),
            jax.ShapeDtypeStruct((rows, feat), BF16),
            jax.ShapeDtypeStruct((rows, feat), BF16),
        ],
        compiler_params=pltpu.CompilerParams(vmem_limit_bytes=VMEM_BYTES),
        cost_estimate=pl.CostEstimate(
            flops=6 * rows * width * feat,
            bytes_accessed=4 * rows * width + 6 * width * feat + 12 * rows * feat,
            transcendentals=0,
        ),
    )(slot, c, dgate, dup, w_gate, w_up, w_down)


def expert_grads(lhs, rights, parts):
    rows, width = lhs.shape
    feat = rights[0].shape[1]
    number = len(rights)
    cols = width // parts
    thin = pl.BlockSpec((rows, feat), lambda i: (0, 0))
    return pl.pallas_call(
        grads_kernel,
        grid=(parts,),
        in_specs=[pl.BlockSpec((rows, cols), lambda i: (0, i))] + [thin] * number,
        out_specs=pl.BlockSpec((1, number, cols, feat), lambda i: (i, 0, 0, 0)),
        out_shape=jax.ShapeDtypeStruct((parts, number, cols, feat), BF16),
        compiler_params=pltpu.CompilerParams(vmem_limit_bytes=VMEM_BYTES),
        cost_estimate=pl.CostEstimate(
            flops=2 * number * rows * width * feat,
            bytes_accessed=2 * rows * width + 2 * number * (width + rows) * feat,
            transcendentals=0,
        ),
    )(lhs, *rights)


def local(tokens, cotangent, expert_ids, combine_weights, w_gate, w_up, w_down, swap_flags):
    tok_rows, width = tokens.shape
    top_count = expert_ids.shape[1]
    per_device = w_gate.shape[0]
    groups = lax.axis_size("expert")
    parts = lax.axis_size("dp")
    half = groups // 2
    experts_all = groups * per_device
    capacity = tok_rows * top_count * 5 // (4 * experts_all) * parts
    total = groups * capacity
    mine = lax.axis_index("dp")
    slot = mine.astype(jnp.int32).reshape(1)

    info = jnp.concatenate([expert_ids.astype(F32), combine_weights], axis=1)
    info = lax.all_gather(info, "dp", tiled=True)
    tok_all = lax.all_gather(tokens, "dp", tiled=True)
    cot_all = lax.all_gather(cotangent, "dp", tiled=True)
    ids = info[:, :top_count].astype(jnp.int32)
    weights = info[:, top_count:]
    count = ids.shape[0]
    wanted = jnp.arange(groups, dtype=jnp.int32) * per_device + mine
    match = ids[:, :, None] == wanted[None, None, :]
    hit = jnp.any(match, axis=1)
    route_weight = jnp.sum(jnp.where(match, weights[:, :, None], 0.0), axis=1)
    below = (jnp.arange(count)[:, None] > jnp.arange(count)[None, :]).astype(BF16)
    rank = dot(below, hit.astype(BF16), ((1,), (0,))).astype(jnp.int32)
    place = jnp.where(hit, rank, -1).T
    picked = place[:, None, :] == jnp.arange(capacity, dtype=jnp.int32)[None, :, None]
    row_weight = jnp.sum(jnp.where(picked, route_weight.T[:, None, :], 0.0), axis=2).reshape(total, 1)
    pick = picked.astype(BF16).reshape(total, count)
    pick_weighted = (
        jnp.where(picked, route_weight.T[:, None, :], 0.0).astype(BF16).reshape(total, count)
    )

    def exchange(value):
        shape = (groups, capacity, width)
        return lax.all_to_all(
            value.reshape(shape), "expert", split_axis=0, concat_axis=0, tiled=True
        ).reshape(total, width)

    x = exchange(dot(pick, tok_all, ((1,), (0,))).astype(BF16))
    c = exchange((dot(pick, cot_all, ((1,), (0,))) * row_weight).astype(BF16))
    out, hidden, dgate, dup = expert_forward(slot, x, w_gate, w_up, w_down)
    out_back = exchange(out)

    def blocks(grads):
        return [
            lax.dynamic_index_in_dim(grads, mine ^ step, keepdims=False) for step in range(parts)
        ]

    def swap(block, step):
        return lax.ppermute(block, "dp", [(i, i ^ step) for i in range(parts)])

    down = blocks(expert_grads(c, [hidden], parts))
    dgate, *down = lax.optimization_barrier((dgate, *down))
    down = down[:1] + [swap(down[step], step) for step in range(1, parts)]
    term, gate_cot, up_cot = expert_backward(slot, c, dgate, dup, w_gate, w_up, w_down)
    both = blocks(expert_grads(x, [gate_cot, up_cot], parts))
    both[0], *moved = lax.optimization_barrier((both[0], *both[1:], *down[1:]))
    both, down = both[:1] + moved[: parts - 1], down[:1] + moved[parts - 1 :]
    both = both[:1] + [swap(both[step], step) for step in range(1, parts)]
    term, *ready = lax.optimization_barrier((term, *down, *both[:-1]))
    term_back = exchange(term)
    term_back, final = lax.optimization_barrier((term_back, both[-1]))
    down, both = ready[:parts], [*ready[parts:], final]
    received = [jnp.concatenate([b, d], axis=0) for b, d in zip(both, down)]

    mixed_part = dot(pick_weighted, out_back, ((0,), (0,))).astype(BF16)
    mixed = lax.psum_scatter(mixed_part, "dp", scatter_dimension=0, tiled=True)
    input_part = dot(pick, term_back, ((0,), (0,))).astype(BF16)
    input_grad = lax.psum_scatter(input_part, "dp", scatter_dimension=0, tiled=True)

    last = lax.select_n((per_device - 1) ^ mine, *received)
    pairs = [(i, (i + half) % groups) for i in range(groups)]
    peer = lax.ppermute(last, "expert", pairs)
    pair = lax.axis_index("expert") % half
    flag = jnp.sum(jnp.where(jnp.arange(half) == pair, swap_flags, 0)) == 1
    chosen = jnp.where(flag, peer, last)
    out_grads = []
    for m in range(3):
        whole = jnp.zeros((per_device,) + last.shape[1:], BF16)
        for step in range(parts):
            whole = lax.dynamic_update_index_in_dim(whole, received[step][m], mine ^ step, 0)
        out_grads.append(whole.at[per_device - 1].set(chosen[m]))
    return (mixed, input_grad, *out_grads)


MESH = pl.DeviceIdType.MESH
KERNEL_VMEM = 62 * 1024 * 1024
STRIPE = 512
LATE = False


def plane_kernel(
    cap,
    tokens, cotangent, names, weighing, wg, wu, wd,
    mixed, igrad, gg, gu, gd, everyone, first, second, acts, peer,
    infos, wgu, wdv, acc_in, acc_down, xs, cs, stage, part, picks, row_weights,
    send_block, send_info, send_z, send_zinfo, recv_column, recv_block, recv_info, send_act, recv_act, act_sem,
    local_sem, stage_sem, send_first, recv_first, send_second, recv_second, send_swap, recv_swap,
):
    parts, groups = everyone.shape[0], everyone.shape[1]
    toks, width = tokens.shape
    own = part.at[0]
    experts, _, feat = wg.shape
    top = names.shape[0]
    cut = width // parts
    rows = experts * 2 * cap
    j = lax.axis_index("expert")
    z = lax.axis_index("dp")
    core = j % 2
    chip = j // 2
    across_x = (j // 4) * 4 + (1 - chip % 2) * 2 + core
    across_y = (1 - j // 4) * 4 + (chip % 2) * 2 + core
    mate = j + 1 - 2 * core
    def near(k):
        swung = core
        return across_x + swung * (across_y - across_x)

    def next_one(k):
        swung = core
        return across_y + swung * (across_x - across_y)

    far = (3 - chip) * 2 + core
    half = z // 2
    outer = z + 1 - 2 * (z % 2)
    inner = 3 - z
    inside = (z + half) % 2

    here = pl.ds(pl.multiple_of(z * cut, cut), cut)

    def plane(k):
        return jnp.where(
            k == 0, z, jnp.where(k == 1, 2 - half, jnp.where(k == 2, 3 - 3 * half, outer))
        )

    barrier = pltpu.get_barrier_semaphore()
    for other in (across_x, across_y, mate):
        pl.semaphore_signal(barrier, inc=1, device_id=(other, z), device_id_type=MESH)
    pl.semaphore_signal(barrier, inc=1, device_id=(j, outer), device_id_type=MESH)

    @pl.when(inside == 1)
    def _():
        pl.semaphore_signal(barrier, inc=1, device_id=(j, inner), device_id_type=MESH)

    locals_ = [
        pltpu.make_async_copy(wg, wgu.at[:, :, pl.ds(0, feat)], local_sem.at[0]),
        pltpu.make_async_copy(wu, wgu.at[:, :, pl.ds(feat, feat)], local_sem.at[1]),
        pltpu.make_async_copy(wd, wdv, local_sem.at[2]),
        pltpu.make_async_copy(tokens, part.at[0, 0], local_sem.at[3]),
        pltpu.make_async_copy(cotangent, part.at[0, 1], local_sem.at[4]),
        pltpu.make_async_copy(own, everyone.at[z, j], local_sem.at[5]),
    ]
    locals_[3].start()
    locals_[4].start()
    infos[z, j, pl.ds(0, top)] = names[...].astype(F32)
    infos[z, j, pl.ds(top, top)] = weighing[...]
    locals_[3].wait()
    locals_[4].wait()
    pl.semaphore_wait(barrier, 4 + inside)

    def remote(src, dst, send, recv, to, row=None):
        return pltpu.make_async_remote_copy(
            src_ref=src, dst_ref=dst, send_sem=send, recv_sem=recv,
            device_id=(to, z if row is None else row), device_id_type=MESH,
        )

    def pass_on(k, kind, zc, block, to, source=None, source_info=None):
        return (
            remote(
                everyone.at[zc, block] if source is None else source,
                everyone.at[zc, block],
                send_block.at[k, kind], recv_block.at[zc, block], to,
            ),
            remote(
                infos.at[zc, block] if source_info is None else source_info,
                infos.at[zc, block],
                send_info.at[k, kind], recv_info.at[zc, block], to,
            ),
        )

    def pass_slice(kind, block, to):
        ref = everyone.at[outer, block, :, :, here]
        return (
            remote(ref, ref, send_block.at[3, kind], recv_block.at[outer, block], to),
            remote(
                infos.at[outer, block], infos.at[outer, block],
                send_info.at[3, kind], recv_info.at[outer, block], to,
            ),
        )

    def send_acts(s):
        return [
            remote(
                ref.at[s, pl.ds(0, groups * cap)], acts.at[m, s],
                send_act.at[m, s], recv_act.at[m, s], j, outer,
            )
            for m, ref in enumerate((gg, gu, gd))
        ]

    def take_acts(s):
        return [
            pltpu.make_async_copy(
                acts.at[m, s], xs.at[s, :, pl.ds(cut + m * feat, feat)], act_sem.at[m, s]
            )
            for m in range(3)
        ]

    def along_z(slot, zc, to, h, source=None):
        return remote(
            everyone.at[zc, j, h] if source is None else source.at[h],
            everyone.at[zc, j, h],
            send_z.at[slot, h], recv_column.at[zc, h], j, to,
        )

    def info_z(slot, zc, to, source=None):
        return remote(
            infos.at[zc, j] if source is None else source,
            infos.at[zc, j],
            send_zinfo.at[slot], recv_info.at[zc, j], j, to,
        )

    def slice_z(zc, source=None):
        there = pl.ds(pl.multiple_of((z + outer - zc) * cut, cut), cut)
        return remote(
            everyone.at[zc, j, :, :, there] if source is None else source.at[:, :, there],
            everyone.at[zc, j, :, :, there],
            send_z.at[0, 0], recv_column.at[zc, 0], j, outer,
        )

    def column_arrived(zc):
        for h in range(2):
            along_z(0, zc, outer, h).wait_recv()
        info_z(0, zc, outer).wait_recv()

    def forward(slot, zc, to):
        info_z(0, zc, outer).wait_recv()
        info_z(slot, zc, to).start()

    def start(pair):
        pair[0].start()
        pair[1].start()

    def arrived(zc, block):
        for copy in pass_on(0, 0, zc, block, mate):
            copy.wait_recv()

    def arrived_slice(block):
        for copy in pass_slice(0, block, mate):
            copy.wait_recv()

    start(pass_on(0, 0, z, j, near(0), own))
    start(pass_on(0, 1, z, j, next_one(0), own))
    info_z(0, z, outer).start()

    @pl.when(inside == 0)
    def _():
        for h in range(2):
            along_z(0, z, outer, h, own).start()

    @pl.when(inside == 1)
    def _():
        slice_z(z, own).start()
        info_z(1, z, inner).start()
        for h in range(2):
            along_z(1, z, inner, h, own).start()

    start(pass_on(0, 3, z, j, mate, own))
    locals_[5].start()
    for copy in locals_[:3]:
        copy.start()
    acc_in[...] = jnp.zeros_like(acc_in)
    acc_down[...] = jnp.zeros_like(acc_down)
    locals_[5].wait()

    def chip_at(k, i):
        return jnp.where(
            i == 0,
            chip,
            jnp.where(i == 1, near(k) // 2, jnp.where(i == 2, next_one(k) // 2, far // 2)),
        )

    def bring(k, i):
        return pltpu.make_async_copy(
            everyone.at[plane(k), pl.ds(2 * chip_at(k, i), 2)], stage.at[i % 2], stage_sem.at[i % 2]
        )

    def bring_slice(i):
        return pltpu.make_async_copy(
            everyone.at[outer, pl.ds(2 * chip_at(3, i), 2), :, :, here],
            stage.at[i % 2, :, :, :, pl.ds(0, cut)],
            stage_sem.at[i % 2],
        )

    def gather(zc, i, at, stripes):
        hits, weights = [], []
        for s in range(experts):
            name = (experts * j + s).astype(F32)
            for b in range(2):
                table = infos[zc, 2 * at + b]
                match = table[:top] == name
                hits.append(jnp.sum(jnp.where(match, 1.0, 0.0), axis=0, keepdims=True))
                weights.append(jnp.sum(jnp.where(match, table[top:], 0.0), axis=0, keepdims=True))
        hit = jnp.concatenate(hits, axis=0)
        before = (
            lax.broadcasted_iota(jnp.int32, (toks, toks), 0)
            < lax.broadcasted_iota(jnp.int32, (toks, toks), 1)
        )
        rank = dot(hit.astype(BF16), jnp.where(before, 1.0, 0.0).astype(BF16), ((1,), (0,)))
        line = lax.broadcasted_iota(jnp.int32, (2 * cap, 2 * toks), 0).astype(F32)
        chosen, scales = [], []
        for s in range(experts):
            place = jnp.concatenate(
                [
                    jnp.where(hits[2 * s + b] > 0, rank[2 * s + b : 2 * s + b + 1] + cap * b, -1.0)
                    for b in range(2)
                ],
                axis=1,
            )
            weight = jnp.concatenate(weights[2 * s : 2 * s + 2], axis=1)
            same = line == place
            chosen.append(jnp.where(same, 1.0, 0.0).astype(BF16))
            scales.append(jnp.sum(jnp.where(same, weight, 0.0), axis=1, keepdims=True))
        pick = jnp.concatenate(chosen, axis=0)
        scale = jnp.concatenate(scales, axis=0)
        picks[i] = pick
        row_weights[i] = scale
        for n in range(stripes):
            cols = pl.ds(n * STRIPE, STRIPE)
            tok = stage[i % 2, :, 0, :, cols].reshape(2 * toks, STRIPE)
            xs[i, :, cols] = dot(pick, tok, ((1,), (0,))).astype(BF16)
            cot = stage[i % 2, :, 1, :, cols].reshape(2 * toks, STRIPE)
            cs[i, :, cols] = (dot(pick, cot, ((1,), (0,))) * scale).astype(BF16)

    def expert(k, s):
        mine = pl.ds(pl.multiple_of(s * 2 * cap, 16), 2 * cap)
        count = groups * cap
        x = xs[:, mine, :].reshape(count, width)
        both = dot(x, wgu[s], ((1,), (0,)))
        c = cs[:, mine, :].reshape(count, width)
        hidden_cot = dot(c, wdv[s], ((1,), (0,)))
        gate, up = both[:, :feat], both[:, feat:]
        sig = jax.nn.sigmoid(gate)
        silu = gate * sig
        hidden = (silu * up).astype(BF16)
        cots = jnp.concatenate(
            [
                (hidden_cot * up * sig * (1.0 + gate * (1.0 - sig))).astype(BF16),
                (hidden_cot * silu).astype(BF16),
            ],
            axis=1,
        )
        acc_in[s] += dot(xs[:, mine, here].reshape(count, cut), cots, ((0,), (0,)))
        acc_down[s] += dot(cs[:, mine, here].reshape(count, cut), hidden, ((0,), (0,)))

        @pl.when(k == 0)
        def _():
            gg[s, pl.ds(0, count)] = cots[:, :feat]
            gu[s, pl.ds(0, count)] = cots[:, feat:]
            gd[s, pl.ds(0, count)] = hidden
            for copy in send_acts(s):
                copy.start()
            scale = row_weights[:, mine, :].reshape(count, 1)
            for n in range(width // STRIPE):
                cols = pl.ds(n * STRIPE, STRIPE)
                out = dot(hidden, wdv[s, cols, :], ((1,), (1,))) * scale
                xs[:, mine, cols] = out.astype(BF16).reshape(groups // 2, 2 * cap, STRIPE)
                term = dot(cots, wgu[s, cols, :], ((1,), (1,)))
                cs[:, mine, cols] = term.astype(BF16).reshape(groups // 2, 2 * cap, STRIPE)

    def swaps():
        last = experts - 1
        return [
            remote(ref.at[last], peer.at[m], send_swap.at[m], recv_swap.at[m], across_y)
            for m, ref in enumerate((gg, gu, gd))
        ]

    def to_mate(i):
        there = (2 * i) % 3 + 3 * (i // 3)
        return remote(
            stage.at[i % 2, 1 - core], first.at[there], send_first.at[i], recv_first.at[there], mate
        )

    def from_mate(i):
        return remote(
            stage.at[i % 2, 1 - core], first.at[i], send_first.at[i], recv_first.at[i], mate
        )

    def combine(i, _):
        @pl.when(i >= 2)
        def _():
            to_mate(i - 2).wait_send()

        for n in range(width // STRIPE):
            cols = pl.ds(n * STRIPE, STRIPE)
            for a, ref in enumerate((xs, cs)):
                total = dot(picks[i], ref[i, :, cols], ((0,), (0,))).astype(BF16)
                stage[i % 2, :, a, :, cols] = total.reshape(2, toks, STRIPE)
        to_mate(i).start()
        part[i] = stage[i % 2, core]
        return 0

    def reduce_copy(which):
        source, to = ((3, near(0)), (1, near(0)), (2, next_one(0)))[which]
        return remote(
            part.at[source], second.at[which], send_second.at[which],
            recv_second.at[which], to,
        )

    def fetch(ref, at, slot):
        copy = pltpu.make_async_copy(ref.at[at], stage.at[slot, 0], stage_sem.at[slot])
        copy.start()
        copy.wait()
        return stage[slot, 0]

    def add_mate():
        def one(i, _):
            from_mate(i).wait_recv()
            got = fetch(first, i, 0)
            part[i] = (part[i].astype(F32) + got.astype(F32)).astype(BF16)
            return 0

        lax.fori_loop(0, groups // 2, one, 0)
        reduce_copy(0).start()
        reduce_copy(1).start()

    def add_relay():
        reduce_copy(0).wait_recv()
        got = fetch(second, 0, 0)
        part[2] = (part[2].astype(F32) + got.astype(F32)).astype(BF16)
        reduce_copy(2).start()

    def column(k):
        zc = plane(k)

        @pl.when(inside == 0)
        def _():
            column_arrived(zc)

        start(pass_on(k, 0, zc, j, near(k)))
        start(pass_on(k, 1, zc, j, next_one(k)))
        start(pass_on(k, 3, zc, j, mate))

    def relay(k):
        zc = plane(k)
        arrived(zc, near(k))
        start(pass_on(k, 2, zc, near(k), next_one(k)))
        start(pass_on(k, 4, zc, near(k), mate))
        arrived(zc, next_one(k))
        start(pass_on(k, 5, zc, next_one(k), mate))

    def slice_relay():
        arrived_slice(near(3))
        start(pass_slice(2, near(3), next_one(3)))
        start(pass_slice(4, near(3), mate))
        arrived_slice(next_one(3))
        start(pass_slice(5, next_one(3), mate))

    @pl.when(inside == 1)
    def _():
        forward(3, inner, outer)
        forward(2, outer, inner)
        for h in range(2):
            along_z(1, inner, outer, h).wait_recv()
            along_z(3, inner, outer, h).start()
            along_z(0, outer, outer, h).wait_recv()
            along_z(2, outer, inner, h).start()

    @pl.when(inside == 0)
    def _():
        slice_z(outer).wait_recv()
        info_z(0, outer, outer).wait_recv()

    relay(0)
    start(pass_slice(0, j, near(3)))
    start(pass_slice(1, j, next_one(3)))
    start(pass_slice(3, j, mate))

    def finish(i, s):
        gg[s] = acc_in[s, :, :feat].astype(BF16)
        gu[s] = acc_in[s, :, feat:].astype(BF16)
        gd[s] = acc_down[s].astype(BF16)

        @pl.when(i == 0)
        def _():
            for copy in swaps():
                copy.start()

    def slice_chunk():
        arrived_slice(mate)
        bring_slice(0).start()

        def pair(i, _):
            @pl.when(i < groups // 2 - 1)
            def _():
                arrived_slice(2 * chip_at(3, i + 1) + 1 - core)
                bring_slice(i + 1).start()

            bring_slice(i).wait()
            gather(outer, i, chip_at(3, i), cut // STRIPE)
            return 0

        lax.fori_loop(0, groups // 2, pair, 0)

        def take(i, _):
            s = experts - 1 - i
            for copy in send_acts(s):
                copy.wait_recv()
            for copy in take_acts(s):
                copy.start()
            return 0

        lax.fori_loop(0, experts, take, 0)

        def each(i, _):
            s = experts - 1 - i
            for copy in take_acts(s):
                copy.wait()
            mine = pl.ds(pl.multiple_of(s * 2 * cap, 16), 2 * cap)
            count = groups * cap
            x = xs[:, mine, pl.ds(0, cut)].reshape(count, cut)
            c = cs[:, mine, pl.ds(0, cut)].reshape(count, cut)
            acc_in[s] += dot(x, xs[s, :, pl.ds(cut, 2 * feat)], ((0,), (0,)))
            acc_down[s] += dot(c, xs[s, :, pl.ds(cut + 2 * feat, feat)], ((0,), (0,)))
            for copy in send_acts(s):
                copy.wait_send()
            if LATE:
                finish(i, s)
            return 0

        lax.fori_loop(0, experts, each, 0)

    def chunk(k, _):
        zc = plane(k)
        arrived(zc, mate)
        bring(k, 0).start()

        def pair(i, _):
            @pl.when(i == 2)
            def _():
                arrived(zc, far)
                start(pass_on(k, 6, zc, far, mate))

                @pl.when(k == 0)
                def _():
                    column(1)
                    slice_relay()

                    @pl.when(inside == 1)
                    def _():
                        forward(4, plane(2), outer)
                        for h in range(2):
                            along_z(1, plane(2), outer, h).wait_recv()
                            along_z(4, plane(2), outer, h).start()

                @pl.when(k == 1)
                def _():
                    relay(2)
                    arrived_slice(far)
                    start(pass_slice(6, far, mate))

            @pl.when(i < groups // 2 - 1)
            def _():
                arrived(zc, 2 * chip_at(k, i + 1) + 1 - core)
                bring(k, i + 1).start()

            bring(k, i).wait()
            gather(zc, i, chip_at(k, i), width // STRIPE)
            return 0

        lax.fori_loop(0, groups // 2, pair, 0)

        @pl.when(k == 0)
        def _():
            for copy in locals_[:3]:
                copy.wait()


        def each(i, _):
            s = experts - 1 - i
            expert(k, s)

            @pl.when((k == 0) & (i == 1))
            def _():
                relay(1)
                column(2)

            if not LATE:
                @pl.when(k == 2)
                def _():
                    finish(i, s)

            return 0

        lax.fori_loop(0, experts, each, 0)

        @pl.when(k == 0)
        def _():
            for kind in (0, 1, 3):
                for copy in pass_on(0, kind, z, j, mate, own):
                    copy.wait_send()

            @pl.when(inside == 0)
            def _():
                for h in range(2):
                    along_z(0, z, outer, h, own).wait_send()

            @pl.when(inside == 1)
            def _():
                slice_z(z, own).wait_send()
                for h in range(2):
                    along_z(1, z, inner, h, own).wait_send()

            lax.fori_loop(0, groups // 2, combine, 0)
            to_mate(2).wait_send()
            to_mate(3).wait_send()
            add_mate()

        @pl.when(k == 1)
        def _():
            add_relay()
            if not LATE:
                slice_chunk()

        return 0

    lax.fori_loop(0, 3, chunk, 0)
    if LATE:
        slice_chunk()

    for which in (1, 2):
        reduce_copy(which).wait_recv()
    one, two = fetch(second, 1, 0).astype(F32), fetch(second, 2, 1).astype(F32)
    total = (part[0].astype(F32) + one + two).astype(BF16)
    mixed[...] = total[0]
    igrad[...] = total[1]
    for which in range(3):
        reduce_copy(which).wait_send()
    for copy in swaps():
        copy.wait_send()
    for copy in swaps():
        copy.wait_recv()
    for kind in range(7):
        for k in range(3):
            if k or kind not in (0, 1, 3):
                for copy in pass_on(k, kind, z, j, mate):
                    copy.wait_send()
        for copy in pass_slice(kind, j, mate):
            copy.wait_send()
    info_z(0, z, outer).wait_send()

    @pl.when(inside == 1)
    def _():
        for slot in range(1, 5):
            info_z(slot, z, outer).wait_send()
        for slot in range(2, 5):
            for h in range(2):
                along_z(slot, z, outer, h).wait_send()


def settle_kernel(flag, mixed, igrad, gg, gu, gd, peer, out_mixed, out_igrad, *outs):
    out_mixed[...] = mixed[...]
    out_igrad[...] = igrad[...]
    moved = (pl.program_id(0) == pl.num_programs(0) - 1) & (flag[0] == 1)
    for m, (ref, out) in enumerate(zip((gg, gu, gd), outs)):
        out[...] = ref[...]

        @pl.when(moved)
        def _():
            out[...] = peer[m]


def local_plane(tokens, cotangent, expert_ids, combine_weights, w_gate, w_up, w_down, swap_flags):
    toks, width = tokens.shape
    top = expert_ids.shape[1]
    experts, _, feat = w_gate.shape
    groups = lax.axis_size("expert")
    parts = lax.axis_size("dp")
    cap = toks * top * 5 // (4 * groups * experts)
    cut = width // parts
    rows = experts * 2 * cap
    chips = groups // 2
    hbm = pl.BlockSpec(memory_space=pltpu.HBM)
    vmem = pl.BlockSpec(memory_space=pltpu.VMEM)
    sem = pltpu.SemaphoreType.DMA
    grad = jax.ShapeDtypeStruct((experts, cut, feat), BF16)
    out = jax.ShapeDtypeStruct((toks, width), BF16)
    results = pl.pallas_call(
        functools.partial(plane_kernel, cap),
        in_specs=[hbm, hbm, vmem, vmem, hbm, hbm, hbm],
        out_specs=[vmem] * 5 + [hbm] * 5,
        out_shape=[
            out, out, grad, grad, grad,
            jax.ShapeDtypeStruct((parts, groups, 2, toks, width), BF16),
            jax.ShapeDtypeStruct((chips, 2, toks, width), BF16),
            jax.ShapeDtypeStruct((3, 2, toks, width), BF16),
            jax.ShapeDtypeStruct((3, experts, groups * cap, feat), BF16),
            jax.ShapeDtypeStruct((3, cut, feat), BF16),
        ],
        scratch_shapes=[
            pltpu.VMEM((parts, groups, 2 * top, toks), F32),
            pltpu.VMEM((experts, width, 2 * feat), BF16),
            pltpu.VMEM((experts, width, feat), BF16),
            pltpu.VMEM((experts, cut, 2 * feat), F32),
            pltpu.VMEM((experts, cut, feat), F32),
            pltpu.VMEM((chips, rows, width), BF16),
            pltpu.VMEM((chips, rows, width), BF16),
            pltpu.VMEM((2, 2, 2, toks, width), BF16),
            pltpu.VMEM((chips, 2, toks, width), BF16),
            pltpu.VMEM((chips, rows, 2 * toks), BF16),
            pltpu.VMEM((chips, rows, 1), F32),
            sem((parts, 7)), sem((parts, 7)), sem((5, 2)), sem((5,)), sem((parts, 2)),
            sem((parts, groups)), sem((parts, groups)),
            sem((3, experts)), sem((3, experts)), sem((3, experts)),
            sem((6,)), sem((2,)), sem((chips,)), sem((chips,)),
            sem((3,)), sem((3,)), sem((3,)), sem((3,)),
        ],
        compiler_params=pltpu.CompilerParams(
            collective_id=0, has_side_effects=True, vmem_limit_bytes=KERNEL_VMEM
        ),
        cost_estimate=pl.CostEstimate(
            flops=60_000_000_000, bytes_accessed=100_000_000, transcendentals=5120 * feat
        ),
    )(tokens, cotangent, expert_ids.T, combine_weights.T, w_gate, w_up, w_down)
    pair = lax.axis_index("expert") % (groups // 2)
    flag = jnp.sum(jnp.where(jnp.arange(groups // 2) == pair, swap_flags, 0))
    lines = pl.BlockSpec((toks // experts, width), lambda i, f: (i, 0))
    panel = pl.BlockSpec((None, cut, feat), lambda i, f: (i, 0, 0))
    whole = pl.BlockSpec((3, cut, feat), lambda i, f: (0, 0, 0))
    return pl.pallas_call(
        settle_kernel,
        grid_spec=pltpu.PrefetchScalarGridSpec(
            num_scalar_prefetch=1,
            grid=(experts,),
            in_specs=[lines, lines, panel, panel, panel, whole],
            out_specs=[lines, lines, panel, panel, panel],
        ),
        out_shape=[out, out, grad, grad, grad],
        compiler_params=pltpu.CompilerParams(vmem_limit_bytes=KERNEL_VMEM),
    )(flag.reshape(1), *results[:5], results[9])


def solution(mesh):
    small = mesh.shape["expert"] == 8 and mesh.shape["dp"] == 4
    return jax.shard_map(
        local_plane if small else local,
        mesh=mesh,
        in_specs=(
            P(("expert", "dp"), None),
            P(("expert", "dp"), None),
            P(("expert", "dp"), None),
            P(("expert", "dp"), None),
            P("expert", None, None),
            P("expert", None, None),
            P("expert", None, None),
            P(),
        ),
        out_specs=(
            P(("expert", "dp"), None),
            P(("expert", "dp"), None),
            P("expert", "dp", None),
            P("expert", "dp", None),
            P("expert", "dp", None),
        ),
        check_vma=False,
    )
```
